32 devices in a mesh: peer: 8 (over z, y), grp: 4 (over x, core).
Axes of the slice: x: 2, y: 2, z: 4, core: 2. Of those that a mesh axis runs over, the one named last changes fastest.
Arguments:
- tokens: bfloat16 [4096, 2048], P(('peer', 'grp')), may hold values from -6 to 6
- cotangent: bfloat16 [4096, 2048], P(('peer', 'grp')), may hold values from -6 to 6
- expert_ids: int32 [4096, 4], P(('peer', 'grp')), may hold values from 0 to 31, all different within a row; in each aligned block of 128 rows (0 to 127, 128 to 255, ...) at most 32 rows name the same one
- route_prob: float32 [4096, 4], P(('peer', 'grp')), may hold values from 0.1 to 1
- w_gate: bfloat16 [8, 2048, 704], P('peer', None, 'grp'), may hold values from -0.125 to 0.125
- w_up: bfloat16 [8, 2048, 704], P('peer', None, 'grp'), may hold values from -0.125 to 0.125
- w_down: bfloat16 [8, 704, 2048], P('peer', 'grp'), may hold values from -0.21875 to 0.21875
- student_logits: bfloat16 [8, 8, 151936], P('peer', None, 'grp'), may hold values from -24 to 252
- stale_logits: bfloat16 [8, 8, 151936], P('peer', None, 'grp'), may hold values from -24 to 252
- labels: int32 [8, 8], P('peer'), may hold values from 0 to 151935
Outputs:
- layer_out: bfloat16 [4096, 2048], P(('peer', 'grp'))
- input_grad: bfloat16 [4096, 2048], P(('peer', 'grp'))
- prob_grad: float32 [4096, 4], P(('peer', 'grp'))
- distill_loss: float32 [8, 8], P('peer')
- logit_grad: bfloat16 [8, 8, 151936], P('peer', None, 'grp')
The draws below stay inside these ranges and needn't reach their ends.
Inputs may be any that keep to these rules, and one draw needn't show every extreme that they name: `expert_ids`: each row names 4 different experts; the rows of one device name any one expert at most 32 times.
All inputs are finite; a program needn't handle non-finite values.
Results may differ from the reference program's by a relative error of at most 0.0064.
Values may be sent and summed in bfloat16 or wider, within the bound.
No kernel may reach another device: no remote copies, remote signals or barrier semaphores. Data moves between devices by JAX's collectives and lax.ppermute only.
A program may use at most 64 MiB of HBM per device.

```python
import math
import jax
import jax.numpy as jnp
import numpy as np
from jax import lax

D = 2048
VOCAB = 151936
TOPK = 4
EXPERTS = 32
HID = 704
PIECES = 4
TOK_DEV = 128
LROWS = 8
CAP = 32
FF_PIECE = 176
PEERS = 8
TOKENS = 4096
COLS = 704
N_PEER = 8
N_GRP = 4


def logit_field(key, salt_value):
    key = jax.random.fold_in(key, salt_value)
    key_list = jax.random.split(key, 1)
    logit_shape = (PEERS, LROWS, VOCAB)
    scores = jnp.clip(4.0 * jax.random.normal(key_list[0], logit_shape, jnp.float32), -24.0, 24.0)
    return scores


def draw_student_logits(key, part):
    return logit_field(key, 101).astype(jnp.bfloat16)


def draw_stale_logits(key, part):
    return logit_field(key, 202).astype(jnp.bfloat16)


def plant(values, rng, smallest, top_value):
    spot = [jax.random.randint(jax.random.fold_in(rng, axis), (), 0, length) for axis, length in enumerate(values.shape)]
    longest = values.shape.index(max(values.shape))
    next_to = spot[:longest] + [(spot[longest] + 1) % values.shape[longest]] + spot[longest + 1:]
    return values.at[tuple(spot)].set(smallest).at[tuple(next_to)].set(top_value)


def steps_of(stream_key, dims, cuts, smallest, largest):
    def one(dim, shards_of):
        draws = jax.random.uniform(jax.random.fold_in(jax.random.fold_in(stream_key, 6), dim), (shards_of,), jnp.float32, smallest / len(cuts), largest / len(cuts))
        return jnp.repeat(jnp.exp(draws), dims[dim] // shards_of).reshape((-1,) + (1,) * (len(dims) - dim - 1))

    loudness = one(*cuts[0])
    for cut in cuts[1:]:
        loudness = loudness * one(*cut)
    return loudness


def routed_block(stream_key, own, number, rows, count, top, limit, lean):
    ranking = jax.random.permutation(stream_key, count)
    crowded, common = shares(count, rows * top, limit, lean, True), shares(count, rows * top, limit, lean, False)
    places = jnp.arange(count)

    def named(sizes, rotation):
        used = int((sizes > 0).sum())
        fixed = max(1, used // 4)
        passed = fixed + (places - fixed + rotation * (used - fixed)) % max(1, count - fixed)
        return jnp.zeros((count,), jnp.int32).at[ranking[jnp.where(places < fixed, places, passed)]].set(jnp.asarray(sizes, jnp.int32))

    sizes = jnp.where(number % 4 == 0, named(crowded, number // 4), named(common, number - number // 4 - 1))
    mixed = jax.random.permutation(jax.random.fold_in(own, 3), count)
    giver, taker = mixed[0:count // 2 * 2:2], mixed[1:count // 2 * 2:2]
    room = jnp.minimum(sizes[giver] - 1, limit - sizes[taker]) // 2
    room = jnp.where((giver == ranking[0]) | (taker == ranking[0]) | (sizes[taker] == 0), 0, jnp.maximum(room, 0))
    passed = jax.random.randint(jax.random.fold_in(own, 4), (count // 2,), 0, 1 << 20) % (room + 1)
    sizes = sizes.at[giver].add(-passed).at[taker].add(passed)
    members = jnp.searchsorted(jnp.cumsum(sizes), jnp.arange(rows * top), side="right").astype(jnp.int32)
    grid = members.reshape(top, rows).T
    grid = grid[jax.random.permutation(jax.random.fold_in(own, 1), rows)]
    rotation = jax.random.randint(jax.random.fold_in(own, 2), (rows, 1), 0, top)
    return jnp.take_along_axis(grid, (jnp.arange(top)[None, :] + rotation) % top, axis=1)


def shares(count, total, reach, skew, full):
    loads = [(1 << 20) // math.isqrt(grade ** skew) + 1 for grade in range(1, count + 1)]
    largest = reach if full else min(reach, max(-(-total // count), total * loads[0] // sum(loads)))
    least = 1 if total - largest >= count - 1 else 0
    given, rest = [largest] + [least] * (count - 1), total - largest - least * (count - 1)
    while rest > 0:
        free = [i for i in range(1, count) if given[i] < largest] or [i for i in range(1, count) if given[i] < reach]
        whole, remaining = sum([loads[i] for i in free]), rest
        for i in free:
            more = min(reach - given[i], max(1, remaining * loads[i] // whole), rest)
            given[i] = given[i] + more
            rest = rest - more
    return np.array(given)


def noise(rng, shape, scale, most, shards=(), kind=jnp.bfloat16):
    values = scale * jax.random.normal(rng, shape, jnp.float32)
    if shards:
        values = values * steps_of(rng, shape, shards, -0.22, 0.18)
    return jnp.clip(values, -most, most).astype(kind)


def setup_inputs(seed: int = 0) -> dict:
    streams_of = jax.random.split(jax.random.key(seed), 11)
    tokens = noise(streams_of[0], (TOKENS, D), 1.0, 6.0, ((0, 32),))
    cotangent = noise(streams_of[1], (TOKENS, D), 1.0, 6.0, ((0, 32),))
    expert_ids_keys = jax.random.split(jax.random.fold_in(streams_of[2], 1), TOKENS // TOK_DEV)
    expert_ids_turns = jax.random.permutation(jax.random.fold_in(streams_of[2], 3), TOKENS // TOK_DEV)
    expert_ids = jax.vmap(lambda own, number: routed_block(jax.random.fold_in(streams_of[2], 2), own, number, TOK_DEV, EXPERTS, TOPK, CAP, 2))(expert_ids_keys, expert_ids_turns).reshape((TOKENS, TOPK))
    route_prob = jnp.clip(0.1 + 0.9 * jax.random.uniform(streams_of[3], (TOKENS, TOPK), jnp.float32) ** steps_of(streams_of[3], (TOKENS, TOPK), ((0, 32),), -0.2, 0.2), 0.1, 1.0)
    w_gate = noise(streams_of[4], (PEERS, D, COLS), D ** -0.5, 0.125, ((0, 8), (2, 4)))
    w_up = noise(streams_of[5], (PEERS, D, COLS), D ** -0.5, 0.125, ((0, 8), (2, 4)))
    w_down = noise(streams_of[6], (PEERS, COLS, D), HID ** -0.5, 0.21875, ((0, 8), (1, 4)))
    student_logits = draw_student_logits(jax.random.fold_in(streams_of[10], 71), 0)
    stale_logits = draw_stale_logits(jax.random.fold_in(streams_of[10], 71), 0)
    labels = plant(jax.random.randint(streams_of[9], (PEERS, LROWS), 0, VOCAB), jax.random.fold_in(streams_of[9], 1), 0, VOCAB - 1).astype(jnp.int32)
    return {"tokens": tokens, "cotangent": cotangent, "expert_ids": expert_ids, "route_prob": route_prob, "w_gate": w_gate, "w_up": w_up, "w_down": w_down, "student_logits": student_logits, "stale_logits": stale_logits, "labels": labels}


def slot_tables(expert_ids, n_window, capacity):
    window_iota = lax.broadcasted_iota(jnp.int32, (1, 1, n_window), 2)
    member = jnp.sum((expert_ids[:, :, None] == window_iota).astype(jnp.int32), axis=1).astype(jnp.int32)
    position = (jnp.cumsum(member, axis=0) - member).astype(jnp.int32)
    slot_iota = lax.broadcasted_iota(jnp.int32, (1, capacity, 1), 1)
    select = (position.T[:, None, :] == slot_iota) & (member.T[:, None, :] > 0)
    return position, select


def forward_piece(slot_rows, gate_cols, up_cols, down_rows):
    gate_act = jnp.dot(slot_rows, gate_cols, preferred_element_type=jnp.float32)
    up_act = jnp.dot(slot_rows, up_cols, preferred_element_type=jnp.float32)
    hidden = (gate_act * jax.nn.sigmoid(gate_act) * up_act).astype(jnp.bfloat16)
    piece_out = jnp.dot(hidden, down_rows, preferred_element_type=jnp.float32).astype(jnp.bfloat16)
    return piece_out, gate_act, up_act


def backward_piece(scaled_rows, gate_act, up_act, gate_cols, up_cols, down_rows):
    contract = (((1,), (1,)), ((), ()))
    grad_hidden = lax.dot_general(scaled_rows, down_rows, contract, preferred_element_type=jnp.float32)
    sigmoid_gate = jax.nn.sigmoid(gate_act)
    grad_gate = (grad_hidden * up_act * sigmoid_gate * (1.0 + gate_act * (1.0 - sigmoid_gate))).astype(jnp.bfloat16)
    grad_up = (grad_hidden * gate_act * sigmoid_gate).astype(jnp.bfloat16)
    piece_grad = lax.dot_general(grad_gate, gate_cols, contract, preferred_element_type=jnp.float32)
    piece_grad = piece_grad + lax.dot_general(grad_up, up_cols, contract, preferred_element_type=jnp.float32)
    return piece_grad.astype(jnp.bfloat16)


def reference(tokens, cotangent, expert_ids, route_prob, w_gate, w_up, w_down, student_logits, stale_logits, labels):
    n_window = N_GRP // PIECES
    tok_blocks = tokens.reshape(N_PEER, N_GRP, TOK_DEV, D)
    cot_blocks = cotangent.reshape(N_PEER, N_GRP, TOK_DEV, D)
    id_blocks = expert_ids.reshape(N_PEER, N_GRP, TOK_DEV, TOPK)
    prob_blocks = route_prob.reshape(N_PEER, N_GRP, TOK_DEV, TOPK)

    def prepare(src_tokens, src_cot, src_ids, src_prob):
        position, select = slot_tables(src_ids, n_window, CAP)
        select_f = select.astype(jnp.float32)
        window_iota = lax.broadcasted_iota(jnp.int32, (1, 1, n_window), 2)
        token_prob = jnp.sum(src_prob[:, :, None] * (src_ids[:, :, None] == window_iota).astype(jnp.float32), axis=1)
        slot_prob = jnp.einsum("ect,te->ec", select_f, token_prob, precision=lax.Precision.HIGHEST)
        slot_rows = jnp.einsum("ect,td->ecd", select_f, src_tokens.astype(jnp.float32), precision=lax.Precision.HIGHEST).astype(jnp.bfloat16)
        slot_cot = jnp.einsum("ect,td->ecd", select_f, src_cot.astype(jnp.float32), precision=lax.Precision.HIGHEST)
        slot_scaled = (slot_prob[:, :, None] * slot_cot).astype(jnp.bfloat16)
        return slot_rows, slot_scaled, position

    def combine(expert_out, expert_grad, src_ids, src_prob, src_cot, position):
        in_window = src_ids < n_window
        safe_ids = jnp.where(in_window, src_ids, 0).astype(jnp.int32)
        slot_index = jnp.take_along_axis(position, safe_ids, axis=1).astype(jnp.int32)
        flat_index = (safe_ids * CAP + slot_index).astype(jnp.int32)
        out_rows = jnp.where(in_window[:, :, None], jnp.take(expert_out.reshape(-1, D), flat_index, axis=0), 0.0)
        grad_rows = jnp.where(in_window[:, :, None], jnp.take(expert_grad.reshape(-1, D), flat_index, axis=0), 0.0)
        layer_out = jnp.sum(src_prob[:, :, None] * out_rows, axis=1).astype(jnp.bfloat16)
        prob_grad = jnp.sum(src_cot.astype(jnp.float32)[:, None, :] * out_rows, axis=2)
        input_grad = jnp.sum(grad_rows, axis=1).astype(jnp.bfloat16)
        return layer_out, input_grad, prob_grad

    def one_peer(packed):
        peer_tokens, peer_cot, peer_ids, peer_prob, gate_cols, up_cols, down_rows = packed
        slot_rows, slot_scaled, position = jax.vmap(prepare)(peer_tokens, peer_cot, peer_ids, peer_prob)

        def one_piece(piece):
            expert = piece // PIECES
            rows_in = lax.dynamic_index_in_dim(slot_rows, expert, 1, keepdims=False).reshape(-1, D)
            scaled_in = lax.dynamic_index_in_dim(slot_scaled, expert, 1, keepdims=False).reshape(-1, D)
            start = (piece * FF_PIECE).astype(jnp.int32)
            gate_piece = lax.dynamic_slice_in_dim(gate_cols, start, FF_PIECE, 1)
            up_piece = lax.dynamic_slice_in_dim(up_cols, start, FF_PIECE, 1)
            down_piece = lax.dynamic_slice_in_dim(down_rows, start, FF_PIECE, 0)
            piece_out, gate_act, up_act = forward_piece(rows_in, gate_piece, up_piece, down_piece)
            piece_grad = backward_piece(scaled_in, gate_act, up_act, gate_piece, up_piece, down_piece)
            return piece_out, piece_grad

        piece_out, piece_grad = lax.map(one_piece, jnp.arange(N_GRP, dtype=jnp.int32))
        expert_out = jnp.sum(piece_out.astype(jnp.float32).reshape(n_window, PIECES, N_GRP, CAP, D), axis=1)
        expert_grad = jnp.sum(piece_grad.astype(jnp.float32).reshape(n_window, PIECES, N_GRP, CAP, D), axis=1)
        expert_out = jnp.transpose(expert_out, (1, 0, 2, 3))
        expert_grad = jnp.transpose(expert_grad, (1, 0, 2, 3))
        return jax.vmap(combine)(expert_out, expert_grad, peer_ids, peer_prob, peer_cot, position)

    layer_out, input_grad, prob_grad = lax.map(one_peer, (tok_blocks, cot_blocks, id_blocks, prob_blocks, w_gate, w_up, w_down))
    layer_out = layer_out.reshape(TOKENS, D)
    input_grad = input_grad.reshape(TOKENS, D)
    prob_grad = prob_grad.reshape(TOKENS, TOPK)

    student = student_logits.astype(jnp.float32)
    teacher = jnp.roll(stale_logits, 1, axis=0).astype(jnp.float32)
    max_student = jnp.max(student, axis=2, keepdims=True)
    lse_student = max_student + jnp.log(jnp.sum(jnp.exp(student - max_student), axis=2, keepdims=True))
    max_teacher = jnp.max(teacher, axis=2, keepdims=True)
    lse_teacher = max_teacher + jnp.log(jnp.sum(jnp.exp(teacher - max_teacher), axis=2, keepdims=True))
    teacher_prob = jnp.exp(teacher - lse_teacher)
    vocab_iota = lax.broadcasted_iota(jnp.int32, student.shape, 2)
    label_hit = vocab_iota == labels[:, :, None]
    label_logit = jnp.sum(jnp.where(label_hit, student, 0.0), axis=2)
    cross_term = jnp.sum(teacher_prob * (teacher - student), axis=2)
    distill_loss = 2.0 * lse_student[:, :, 0] - label_logit + cross_term - lse_teacher[:, :, 0]
    logit_grad = (2.0 * jnp.exp(student - lse_student) - label_hit.astype(jnp.float32) - teacher_prob).astype(jnp.bfloat16)
    return layer_out, input_grad, prob_grad, distill_loss, logit_grad
```

```python
import functools

import jax
import jax.numpy as jnp
from jax import lax
from jax.experimental import pallas as pl
from jax.experimental.pallas import tpu as pltpu
from jax.sharding import PartitionSpec as P

PIECES = 4
CAP = 32
LANES = 128
CHUNK = 2048
NT = (((1,), (1,)), ((), ()))
TN = (((0,), (0,)), ((), ()))


def vmem(count):
    return [pl.BlockSpec(memory_space=pltpu.VMEM)] * count


def params(mib):
    return pltpu.CompilerParams(vmem_limit_bytes=mib * 1024 * 1024)


def swapped(value, axis, bits):
    count = lax.axis_size(axis)
    return lax.ppermute(value, axis, [(k, k ^ bits) for k in range(count)])


def onward(value, axis):
    count = lax.axis_size(axis)
    return lax.ppermute(value, axis, [(k, (k + 1) % count) for k in range(count)])


def prepare_kernel(n_window, ids, prob, tokens, cot, rows, scaled, slot_cot, select, slot_prob):
    all_ids = ids[...]
    count = all_ids.shape[1]
    before = (
        lax.broadcasted_iota(jnp.int32, (count, count), 0)
        < lax.broadcasted_iota(jnp.int32, (count, count), 1)
    ).astype(jnp.float32).astype(jnp.bfloat16)
    slot = lax.broadcasted_iota(jnp.int32, (CAP, count), 0)
    for e in range(n_window):
        part = pl.ds(e * CAP, CAP)
        hit = all_ids == e
        member = jnp.sum(hit.astype(jnp.float32), axis=0, keepdims=True)
        token_prob = jnp.sum(jnp.where(hit, prob[...], 0.0), axis=0, keepdims=True)
        earlier = jnp.dot(
            jnp.broadcast_to(member, (16, count)).astype(jnp.bfloat16),
            before,
            preferred_element_type=jnp.float32,
        )
        position = earlier[:1].astype(jnp.int32)
        chosen = (slot == position) & (member > 0.5)
        chosen_f = chosen.astype(jnp.float32)
        chosen_b = chosen_f.astype(jnp.bfloat16)
        weight = jnp.sum(chosen_f * token_prob, axis=1, keepdims=True)
        rows[part, :] = jnp.dot(
            chosen_b, tokens[...], preferred_element_type=jnp.float32
        ).astype(jnp.bfloat16)
        cot_rows = jnp.dot(chosen_b, cot[...], preferred_element_type=jnp.float32)
        slot_cot[part, :] = cot_rows.astype(jnp.bfloat16)
        scaled[part, :] = (weight * cot_rows).astype(jnp.bfloat16)
        select[part, :] = chosen_f
        slot_prob[part, :] = jnp.broadcast_to(weight, (CAP, LANES))


def prepare(ids, prob, tokens, cot, n_window):
    count, width = tokens.shape
    slots = n_window * CAP
    wide = jax.ShapeDtypeStruct((slots, width), jnp.bfloat16)
    return pl.pallas_call(
        functools.partial(prepare_kernel, n_window),
        out_shape=(
            wide,
            wide,
            wide,
            jax.ShapeDtypeStruct((slots, count), jnp.float32),
            jax.ShapeDtypeStruct((slots, LANES), jnp.float32),
        ),
        in_specs=vmem(4),
        out_specs=tuple(vmem(5)),
        compiler_params=params(8),
        name="prepare",
    )(ids, prob, tokens, cot)


def piece_kernel(rows_a, rows_b, scaled_a, scaled_b, gate_w, up_w, down_w, out_a, grad_a, send):
    half = rows_a.shape[0]
    rows = jnp.concatenate([rows_a[...], rows_b[...]], axis=0)
    gate = lax.dot_general(rows, gate_w[...], NT, preferred_element_type=jnp.float32)
    up = lax.dot_general(rows, up_w[...], NT, preferred_element_type=jnp.float32)
    sig = jax.nn.sigmoid(gate)
    hidden = (gate * sig * up).astype(jnp.bfloat16)
    out = jnp.dot(hidden, down_w[...], preferred_element_type=jnp.float32).astype(jnp.bfloat16)
    out_a[...] = out[:half]
    send[:half, :] = out[half:]
    scaled = jnp.concatenate([scaled_a[...], scaled_b[...]], axis=0)
    grad_hidden = lax.dot_general(scaled, down_w[...], NT, preferred_element_type=jnp.float32)
    grad_gate = (grad_hidden * up * sig * (1.0 + gate * (1.0 - sig))).astype(jnp.bfloat16)
    grad_up = (grad_hidden * gate * sig).astype(jnp.bfloat16)
    grad = jnp.dot(grad_gate, gate_w[...], preferred_element_type=jnp.float32)
    grad = grad + jnp.dot(grad_up, up_w[...], preferred_element_type=jnp.float32)
    grad = grad.astype(jnp.bfloat16)
    grad_a[...] = grad[:half]
    send[half:, :] = grad[half:]


def piece(rows_a, rows_b, scaled_a, scaled_b, gate_w, up_w, down_w):
    half, width = rows_a.shape
    return pl.pallas_call(
        piece_kernel,
        out_shape=(
            jax.ShapeDtypeStruct((half, width), jnp.bfloat16),
            jax.ShapeDtypeStruct((half, width), jnp.bfloat16),
            jax.ShapeDtypeStruct((2 * half, width), jnp.bfloat16),
        ),
        in_specs=vmem(7),
        out_specs=tuple(vmem(3)),
        compiler_params=params(16),
        name="piece",
    )(rows_a, rows_b, scaled_a, scaled_b, gate_w, up_w, down_w)


def spread(select, value, exact):
    high = value.astype(jnp.bfloat16)
    chosen = select.astype(jnp.bfloat16)
    total = lax.dot_general(chosen, high, TN, preferred_element_type=jnp.float32)
    if exact:
        return total
    low = (value - high.astype(jnp.float32)).astype(jnp.bfloat16)
    return total + lax.dot_general(chosen, low, TN, preferred_element_type=jnp.float32)


def combine_kernel(n_window, parts, *refs):
    outs, grads = refs[:parts], refs[parts : 2 * parts]
    ids, select, slot_prob, slot_cot, layer_out, input_grad, prob_grad = refs[2 * parts :]
    exact = n_window == 1
    out = outs[0][...].astype(jnp.float32)
    for other in outs[1:]:
        out = out + other[...].astype(jnp.float32)
    chosen = select[...]
    per_slot = jnp.sum(out * slot_cot[...].astype(jnp.float32), axis=1, keepdims=True)
    spread_prob = chosen * per_slot
    for e in range(n_window):
        per_token = jnp.sum(spread_prob[e * CAP : (e + 1) * CAP], axis=0, keepdims=True)
        kept = jnp.where(ids[...] == e, per_token, 0.0)
        whole = kept if e == 0 else whole + kept
    prob_grad[...] = whole
    weighted = slot_prob[:, :1] * out
    layer_out[...] = spread(chosen, weighted, exact).astype(jnp.bfloat16)
    grad = grads[0][...].astype(jnp.float32)
    for other in grads[1:]:
        grad = grad + other[...].astype(jnp.float32)
    input_grad[...] = spread(chosen, grad, exact).astype(jnp.bfloat16)


def combine(outs, grads, ids, select, slot_prob, slot_cot, n_window):
    parts = len(outs)
    width = outs[0].shape[1]
    topk, count = ids.shape
    return pl.pallas_call(
        functools.partial(combine_kernel, n_window, parts),
        out_shape=(
            jax.ShapeDtypeStruct((count, width), jnp.bfloat16),
            jax.ShapeDtypeStruct((count, width), jnp.bfloat16),
            jax.ShapeDtypeStruct((topk, count), jnp.float32),
        ),
        in_specs=vmem(2 * parts + 4),
        out_specs=tuple(vmem(3)),
        compiler_params=params(12),
        name="combine",
    )(*outs, *grads, ids, select, slot_prob, slot_cot)


def pieces_of(width):
    full = width // CHUNK
    return full, full * CHUNK, width - full * CHUNK


def over_columns(width, carry, step):
    full, start, rest = pieces_of(width)

    def lap(k, so_far):
        return step(pl.multiple_of(k * CHUNK, CHUNK), CHUNK, so_far)

    if full:
        carry = lax.fori_loop(0, full, lap, carry, unroll=True)
    return carry, start, rest


def row_max(ref, width):
    rows = ref.shape[0]

    def step(at, size, so_far):
        return jnp.maximum(so_far, ref[:, pl.ds(at, size)].astype(jnp.float32))

    top, start, rest = over_columns(
        width, jnp.full((rows, CHUNK), -jnp.inf, jnp.float32), step
    )
    top = jnp.max(top, axis=1, keepdims=True)
    if rest:
        tail = ref[:, start : start + rest].astype(jnp.float32)
        top = jnp.maximum(top, jnp.max(tail, axis=1, keepdims=True))
    return top


def columns(values, rows):
    lane = lax.broadcasted_iota(jnp.int32, (rows, LANES), 1)
    tile = jnp.zeros((rows, LANES), jnp.float32)
    for k, value in enumerate(values):
        tile = jnp.where(lane == k, value, tile)
    return tile


def label_column(labels, base):
    rows = labels.shape[1]
    own = lax.broadcasted_iota(jnp.int32, (rows, rows), 0) == lax.broadcasted_iota(
        jnp.int32, (rows, rows), 1
    )
    spread_out = jnp.where(own, jnp.broadcast_to(labels[...], (rows, rows)), 0)
    return jnp.sum(spread_out.astype(jnp.float32), axis=1, keepdims=True).astype(jnp.int32) - base


def student_kernel(base, labels, student, stats):
    rows, width = student.shape
    top = row_max(student, width)
    label = label_column(labels, base[0])

    def step(at, size, so_far):
        total, picked = so_far
        value = student[:, pl.ds(at, size)].astype(jnp.float32)
        here = lax.broadcasted_iota(jnp.int32, (rows, size), 1) == label - at
        return total + jnp.exp(value - top), picked + jnp.where(here, value, 0.0)

    zero = jnp.zeros((rows, CHUNK), jnp.float32)
    (total, picked), start, rest = over_columns(width, (zero, zero), step)
    total = jnp.sum(total, axis=1, keepdims=True)
    picked = jnp.sum(picked, axis=1, keepdims=True)
    if rest:
        none = jnp.zeros((rows, rest), jnp.float32)
        more, seen = step(start, rest, (none, none))
        total = total + jnp.sum(more, axis=1, keepdims=True)
        picked = picked + jnp.sum(seen, axis=1, keepdims=True)
    stats[...] = columns((top, total, picked), rows)


def teacher_kernel(student, teacher, student_stats, stats):
    rows, width = student.shape
    top = row_max(teacher, width)

    def step(at, size, so_far):
        total, cross = so_far
        ours = student[:, pl.ds(at, size)].astype(jnp.float32)
        theirs = teacher[:, pl.ds(at, size)].astype(jnp.float32)
        power = jnp.exp(theirs - top)
        return total + power, cross + power * (theirs - ours)

    zero = jnp.zeros((rows, CHUNK), jnp.float32)
    (total, cross), start, rest = over_columns(width, (zero, zero), step)
    total = jnp.sum(total, axis=1, keepdims=True)
    cross = jnp.sum(cross, axis=1, keepdims=True)
    if rest:
        none = jnp.zeros((rows, rest), jnp.float32)
        more, seen = step(start, rest, (none, none))
        total = total + jnp.sum(more, axis=1, keepdims=True)
        cross = cross + jnp.sum(seen, axis=1, keepdims=True)
    first = student_stats[...]
    stats[...] = columns(
        (first[:, 0:1], first[:, 1:2], first[:, 2:3], top, total, cross), rows
    )


def final_kernel(parts, base, labels, student, teacher, *refs):
    stats, (loss, grad) = refs[:parts], refs[parts:]
    rows, width = student.shape
    label = label_column(labels, base[0])
    tiles = [ref[...] for ref in stats]
    top = functools.reduce(jnp.maximum, tiles)
    smax, tmax = top[:, 0:1], top[:, 3:4]
    ssum = tsum = cross = picked = jnp.zeros((rows, 1), jnp.float32)
    for tile in tiles:
        ssum = ssum + tile[:, 1:2] * jnp.exp(tile[:, 0:1] - smax)
        scale = jnp.exp(tile[:, 3:4] - tmax)
        tsum = tsum + tile[:, 4:5] * scale
        cross = cross + tile[:, 5:6] * scale
        picked = picked + tile[:, 2:3]
    lse_s = smax + jnp.log(ssum)
    lse_t = tmax + jnp.log(tsum)
    value = 2.0 * lse_s - picked + cross / tsum - lse_t
    own = lax.broadcasted_iota(jnp.int32, (rows, rows), 0) == lax.broadcasted_iota(
        jnp.int32, (rows, rows), 1
    )
    loss[...] = jnp.sum(jnp.where(own, value, 0.0), axis=0, keepdims=True)

    def step(at, size, so_far):
        ours = student[:, pl.ds(at, size)].astype(jnp.float32)
        theirs = teacher[:, pl.ds(at, size)].astype(jnp.float32)
        here = lax.broadcasted_iota(jnp.int32, (rows, size), 1) == label - at
        result = (
            2.0 * jnp.exp(ours - lse_s) - here.astype(jnp.float32) - jnp.exp(theirs - lse_t)
        )
        grad[:, pl.ds(at, size)] = result.astype(jnp.bfloat16)
        return so_far

    _, start, rest = over_columns(width, 0, step)
    if rest:
        step(start, rest, 0)


def scalar_spec():
    return pl.BlockSpec(memory_space=pltpu.SMEM)


def distill(student, stale, labels):
    rows, width = student.shape
    teacher = onward(stale, "peer")
    base = (lax.axis_index("grp") * width).astype(jnp.int32).reshape(1)
    tile = jax.ShapeDtypeStruct((rows, LANES), jnp.float32)
    own = pl.pallas_call(
        student_kernel,
        out_shape=tile,
        in_specs=[scalar_spec()] + vmem(2),
        out_specs=vmem(1)[0],
        compiler_params=params(8),
        name="student",
    )(base, labels, student)
    stats = pl.pallas_call(
        teacher_kernel,
        out_shape=tile,
        in_specs=vmem(3),
        out_specs=vmem(1)[0],
        compiler_params=params(8),
        name="teacher",
    )(student, teacher, own)
    count = lax.axis_size("grp")
    others = [
        lax.ppermute(stats, "grp", [(k, (k + s) % count) for k in range(count)])
        for s in range(1, count)
    ]
    loss, grad = pl.pallas_call(
        functools.partial(final_kernel, count),
        out_shape=(
            jax.ShapeDtypeStruct((1, rows), jnp.float32),
            jax.ShapeDtypeStruct((rows, width), jnp.bfloat16),
        ),
        in_specs=[scalar_spec()] + vmem(3 + count),
        out_specs=tuple(vmem(2)),
        compiler_params=params(8),
        name="final",
    )(base, labels, student, teacher, stats, *others)
    return loss, grad


def between_blocks(value, n_window):
    if n_window == 1:
        return value
    groups = [[b + PIECES * a for a in range(n_window)] for b in range(PIECES)]
    return lax.all_to_all(
        value, "grp", split_axis=0, concat_axis=0, tiled=True, axis_index_groups=groups
    )


def layer(tokens, cotangent, ids, prob, gate_w, up_w, down_w, n_window):
    rows, scaled, slot_cot, select, slot_prob = prepare(ids, prob, tokens, cotangent, n_window)
    rows = between_blocks(rows, n_window)
    scaled = between_blocks(scaled, n_window)
    half = rows.shape[0]
    pair = jnp.concatenate([rows, scaled], axis=0)
    far = swapped(pair, "grp", 2)
    near = swapped(pair, "grp", 1)
    far_near = swapped(far, "grp", 1)
    weights = (gate_w, up_w, down_w)
    out_a, grad_a, send_a = piece(rows, near[:half], scaled, near[half:], *weights)
    back_a = swapped(send_a, "grp", 1)
    out_b, grad_b, send_b = piece(far[:half], far_near[:half], far[half:], far_near[half:], *weights)
    back_b = swapped(send_b, "grp", 1)
    keep_b = jnp.concatenate([out_b, grad_b], axis=0)
    sum_b = (keep_b.astype(jnp.float32) + back_b.astype(jnp.float32)).astype(jnp.bfloat16)
    home = swapped(sum_b, "grp", 2)
    outs = [out_a, back_a[:half], home[:half]]
    grads = [grad_a, back_a[half:], home[half:]]
    if n_window > 1:
        total = functools.reduce(jnp.add, [part.astype(jnp.float32) for part in outs])
        outs = [between_blocks(total.astype(jnp.bfloat16), n_window)]
        total = functools.reduce(jnp.add, [part.astype(jnp.float32) for part in grads])
        grads = [between_blocks(total.astype(jnp.bfloat16), n_window)]
    return combine(outs, grads, ids, select, slot_prob, slot_cot, n_window)


def body(
    tokens,
    cotangent,
    expert_ids,
    route_prob,
    w_gate,
    w_up,
    w_down,
    student_logits,
    stale_logits,
    labels,
):
    n_window = lax.axis_size("grp") // PIECES
    distill_loss, logit_grad = distill(student_logits[0], stale_logits[0], labels)
    layer_out, input_grad, prob_grad = layer(
        tokens,
        cotangent,
        expert_ids.T,
        route_prob.T,
        w_gate[0].T,
        w_up[0].T,
        w_down[0],
        n_window,
    )
    return (layer_out, input_grad, prob_grad.T, distill_loss, logit_grad[None])


def solution(mesh):
    placed = (
        P(("peer", "grp"), None),
        P(("peer", "grp"), None),
        P(("peer", "grp"), None),
        P(("peer", "grp"), None),
        P("peer", None, "grp"),
        P("peer", None, "grp"),
        P("peer", "grp", None),
        P("peer", None, "grp"),
        P("peer", None, "grp"),
        P("peer", None),
    )
    return jax.shard_map(
        body,
        mesh=mesh,
        in_specs=placed,
        out_specs=(
            P(("peer", "grp"), None),
            P(("peer", "grp"), None),
            P(("peer", "grp"), None),
            P("peer", None),
            P("peer", None, "grp"),
        ),
        check_vma=False,
    )
```

```python
import functools

import jax
import jax.numpy as jnp
from jax import lax
from jax.experimental import pallas as pl
from jax.experimental.pallas import tpu as pltpu
from jax.sharding import PartitionSpec as P


PIECES = 4
CAP = 32
LANES = 128
CHUNK = 2048
NT = (((1,), (1,)), ((), ()))
TN = (((0,), (0,)), ((), ()))


def vmem(count):
    return [pl.BlockSpec(memory_space=pltpu.VMEM)] * count


def hbm(count):
    return [pl.BlockSpec(memory_space=pltpu.HBM)] * count


def in_hbm(*values):
    return [pltpu.with_memory_space_constraint(value, pltpu.HBM) for value in values]


def params(mib):
    return pltpu.CompilerParams(vmem_limit_bytes=mib * 1024 * 1024)


def swapped(value, axis, bits):
    count = lax.axis_size(axis)
    return lax.ppermute(value, axis, [(k, k ^ bits) for k in range(count)])


def onward(value, axis):
    count = lax.axis_size(axis)
    return lax.ppermute(value, axis, [(k, (k + 1) % count) for k in range(count)])


def fetched(sources, buffers, sems):
    copies = [
        pltpu.make_async_copy(source, buffer, sems.at[k])
        for k, (source, buffer) in enumerate(zip(sources, buffers))
    ]
    for copy in copies:
        copy.start()
    return copies


def prepare_kernel(
    n_window,
    ids_hbm,
    prob_hbm,
    tokens_hbm,
    cot_hbm,
    rows,
    scaled,
    slot_cot,
    select,
    slot_prob,
    ids_out,
    ids,
    prob,
    tokens,
    cot,
    sems,
):
    copies = fetched(
        (ids_hbm, prob_hbm, tokens_hbm, cot_hbm), (ids, prob, tokens, cot), sems
    )
    copies[0].wait()
    copies[1].wait()
    all_ids = ids[...]
    ids_out[...] = all_ids
    count = all_ids.shape[1]
    before = (
        lax.broadcasted_iota(jnp.int32, (count, count), 0)
        < lax.broadcasted_iota(jnp.int32, (count, count), 1)
    ).astype(jnp.float32).astype(jnp.bfloat16)
    slot = lax.broadcasted_iota(jnp.int32, (CAP, count), 0)
    for e in range(n_window):
        part = pl.ds(e * CAP, CAP)
        hit = all_ids == e
        member = jnp.sum(hit.astype(jnp.float32), axis=0, keepdims=True)
        token_prob = jnp.sum(jnp.where(hit, prob[...], 0.0), axis=0, keepdims=True)
        earlier = jnp.dot(
            jnp.broadcast_to(member, (16, count)).astype(jnp.bfloat16),
            before,
            preferred_element_type=jnp.float32,
        )
        position = earlier[:1].astype(jnp.int32)
        chosen = (slot == position) & (member > 0.5)
        chosen_f = chosen.astype(jnp.float32)
        chosen_b = chosen_f.astype(jnp.bfloat16)
        weight = jnp.sum(chosen_f * token_prob, axis=1, keepdims=True)
        if e == 0:
            copies[2].wait()
        rows[part, :] = jnp.dot(
            chosen_b, tokens[...], preferred_element_type=jnp.float32
        ).astype(jnp.bfloat16)
        if e == 0:
            copies[3].wait()
        cot_rows = jnp.dot(chosen_b, cot[...], preferred_element_type=jnp.float32)
        slot_cot[part, :] = cot_rows.astype(jnp.bfloat16)
        scaled[part, :] = (weight * cot_rows).astype(jnp.bfloat16)
        select[part, :] = chosen_f
        slot_prob[part, :] = jnp.broadcast_to(weight, (CAP, LANES))


def prepare(ids, prob, tokens, cot, n_window):
    count, width = tokens.shape
    slots = n_window * CAP
    wide = jax.ShapeDtypeStruct((slots, width), jnp.bfloat16)
    return pl.pallas_call(
        functools.partial(prepare_kernel, n_window),
        out_shape=(
            wide,
            wide,
            wide,
            jax.ShapeDtypeStruct((slots, count), jnp.float32),
            jax.ShapeDtypeStruct((slots, LANES), jnp.float32),
            jax.ShapeDtypeStruct(ids.shape, ids.dtype),
        ),
        in_specs=hbm(4),
        out_specs=tuple(vmem(6)),
        scratch_shapes=[
            pltpu.VMEM(ids.shape, ids.dtype),
            pltpu.VMEM(prob.shape, prob.dtype),
            pltpu.VMEM(tokens.shape, tokens.dtype),
            pltpu.VMEM(cot.shape, cot.dtype),
            pltpu.SemaphoreType.DMA((4,)),
        ],
        compiler_params=params(8),
        name="prepare",
    )(*in_hbm(ids, prob, tokens, cot))


def forward_math(rows, gate_w, up_w, down_w):
    gate = lax.dot_general(rows, gate_w[...], NT, preferred_element_type=jnp.float32)
    up = lax.dot_general(rows, up_w[...], NT, preferred_element_type=jnp.float32)
    hidden = (gate * jax.nn.sigmoid(gate) * up).astype(jnp.bfloat16)
    out = jnp.dot(hidden, down_w[...], preferred_element_type=jnp.float32)
    return out.astype(jnp.bfloat16), gate, up


def backward_math(scaled, gate, up, gate_w, up_w, down_w):
    sig = jax.nn.sigmoid(gate)
    grad_hidden = lax.dot_general(scaled, down_w[...], NT, preferred_element_type=jnp.float32)
    grad_gate = (grad_hidden * up * sig * (1.0 + gate * (1.0 - sig))).astype(jnp.bfloat16)
    grad_up = (grad_hidden * gate * sig).astype(jnp.bfloat16)
    grad = jnp.dot(grad_gate, gate_w[...], preferred_element_type=jnp.float32)
    grad = grad + jnp.dot(grad_up, up_w[...], preferred_element_type=jnp.float32)
    return grad.astype(jnp.bfloat16)


def forward_kernel(rows_a, rows_b, gate_w, up_w, down_w, keep, send, gate_ref, up_ref):
    half = rows_a.shape[0]
    rows = jnp.concatenate([rows_a[...], rows_b[...]], axis=0)
    out, gate, up = forward_math(rows, gate_w, up_w, down_w)
    keep[...] = out[:half]
    send[...] = out[half:]
    gate_ref[...] = gate
    up_ref[...] = up


def backward_kernel(scaled_a, scaled_b, gate, up, gate_w, up_w, down_w, keep, send):
    half = scaled_a.shape[0]
    scaled = jnp.concatenate([scaled_a[...], scaled_b[...]], axis=0)
    grad = backward_math(scaled, gate[...], up[...], gate_w, up_w, down_w)
    keep[...] = grad[:half]
    send[...] = grad[half:]


def forward(rows_a, rows_b, weights):
    half, width = rows_a.shape
    hidden = weights[0].shape[0]
    part = jax.ShapeDtypeStruct((half, width), jnp.bfloat16)
    act = jax.ShapeDtypeStruct((2 * half, hidden), jnp.float32)
    return pl.pallas_call(
        forward_kernel,
        out_shape=(part, part, act, act),
        in_specs=vmem(5),
        out_specs=tuple(vmem(4)),
        compiler_params=params(12),
        name="forward",
    )(rows_a, rows_b, *weights)


def backward(scaled_a, scaled_b, gate, up, weights):
    half, width = scaled_a.shape
    part = jax.ShapeDtypeStruct((half, width), jnp.bfloat16)
    return pl.pallas_call(
        backward_kernel,
        out_shape=(part, part),
        in_specs=vmem(7),
        out_specs=tuple(vmem(2)),
        compiler_params=params(12),
        name="backward",
    )(scaled_a, scaled_b, gate, up, *weights)


def spread(select, value, exact):
    high = value.astype(jnp.bfloat16)
    chosen = select.astype(jnp.bfloat16)
    total = lax.dot_general(chosen, high, TN, preferred_element_type=jnp.float32)
    if exact:
        return total
    low = (value - high.astype(jnp.float32)).astype(jnp.bfloat16)
    return total + lax.dot_general(chosen, low, TN, preferred_element_type=jnp.float32)


BLOCK = 512


def summed(refs, part):
    total = refs[0][:, part].astype(jnp.float32)
    for other in refs[1:]:
        total = total + other[:, part].astype(jnp.float32)
    return total


def combine_out_kernel(n_window, parts, *refs):
    outs = refs[:parts]
    ids, select, slot_prob, slot_cot, layer_out, prob_grad, stage, prob_stage, sems = refs[parts:]
    exact = n_window == 1
    chosen = select[...]
    weight = slot_prob[:, :1]
    width = outs[0].shape[1]
    block = min(BLOCK, width)
    blocks = width // block
    copies = []
    per_slot = jnp.zeros((chosen.shape[0], 1), jnp.float32)
    for k in range(blocks):
        part = pl.ds(k * block, block)
        out = summed(outs, part)
        per_slot = per_slot + jnp.sum(
            out * slot_cot[:, part].astype(jnp.float32), axis=1, keepdims=True
        )
        stage[:, part] = spread(chosen, weight * out, exact).astype(jnp.bfloat16)
        copy = pltpu.make_async_copy(stage.at[:, part], layer_out.at[:, part], sems.at[k])
        copy.start()
        copies.append(copy)
    spread_prob = chosen * per_slot
    for e in range(n_window):
        per_token = jnp.sum(spread_prob[e * CAP : (e + 1) * CAP], axis=0, keepdims=True)
        kept = jnp.where(ids[...] == e, per_token, 0.0)
        whole = kept if e == 0 else whole + kept
    prob_stage[...] = whole
    copy = pltpu.make_async_copy(prob_stage, prob_grad, sems.at[blocks])
    copy.start()
    copies.append(copy)
    for copy in copies:
        copy.wait()


def combine_grad_kernel(n_window, parts, *refs):
    grads = refs[:parts]
    select, input_grad, stage, sems = refs[parts:]
    exact = n_window == 1
    chosen = select[...]
    width = grads[0].shape[1]
    block = min(BLOCK, width)
    copies = []
    for k in range(width // block):
        part = pl.ds(k * block, block)
        stage[:, part] = spread(chosen, summed(grads, part), exact).astype(jnp.bfloat16)
        copy = pltpu.make_async_copy(stage.at[:, part], input_grad.at[:, part], sems.at[k])
        copy.start()
        copies.append(copy)
    for copy in copies:
        copy.wait()


def combine_out(outs, ids, select, slot_prob, slot_cot, n_window):
    parts = len(outs)
    width = outs[0].shape[1]
    topk, count = ids.shape
    return pl.pallas_call(
        functools.partial(combine_out_kernel, n_window, parts),
        out_shape=(
            jax.ShapeDtypeStruct((count, width), jnp.bfloat16),
            jax.ShapeDtypeStruct((topk, count), jnp.float32),
        ),
        in_specs=vmem(parts + 4),
        out_specs=tuple(hbm(2)),
        scratch_shapes=[
            pltpu.VMEM((count, width), jnp.bfloat16),
            pltpu.VMEM((topk, count), jnp.float32),
            pltpu.SemaphoreType.DMA((width // min(BLOCK, width) + 1,)),
        ],
        compiler_params=params(12),
        name="combine_out",
    )(*outs, ids, select, slot_prob, slot_cot)


def combine_grad(grads, select, n_window):
    parts = len(grads)
    width = grads[0].shape[1]
    count = select.shape[1]
    return pl.pallas_call(
        functools.partial(combine_grad_kernel, n_window, parts),
        out_shape=jax.ShapeDtypeStruct((count, width), jnp.bfloat16),
        in_specs=vmem(parts + 1),
        out_specs=hbm(1)[0],
        scratch_shapes=[
            pltpu.VMEM((count, width), jnp.bfloat16),
            pltpu.SemaphoreType.DMA((width // min(BLOCK, width),)),
        ],
        compiler_params=params(12),
        name="combine_grad",
    )(*grads, select)


def spans(width, parts):
    step = CHUNK * max(1, width // (parts * CHUNK))
    return [(start, min(step, width - start)) for start in range(0, width, step)]


def chunks(start, size):
    return [(at, min(CHUNK, start + size - at)) for at in range(start, start + size, CHUNK)]


def load(ref, at, size):
    return ref[:, pl.ds(at, size)].astype(jnp.float32)


def row_max(ref, start, size, top):
    full = None
    for at, span in chunks(start, size):
        value = load(ref, at, span)
        if span < CHUNK:
            top = jnp.maximum(top, jnp.max(value, axis=1, keepdims=True))
        else:
            full = value if full is None else jnp.maximum(full, value)
    if full is not None:
        top = jnp.maximum(top, jnp.max(full, axis=1, keepdims=True))
    return top


def row_sums(width, step):
    full = tail = None
    for at, span in chunks(0, width):
        values = step(at, span)
        if span < CHUNK:
            tail = values
        elif full is None:
            full = values
        else:
            full = tuple(one + two for one, two in zip(full, values))
    sums = [jnp.sum(value, axis=1, keepdims=True) for value in (full or tail)]
    if full is not None and tail is not None:
        more = [jnp.sum(value, axis=1, keepdims=True) for value in tail]
        sums = [one + two for one, two in zip(sums, more)]
    return sums


def columns(values, rows):
    lane = lax.broadcasted_iota(jnp.int32, (rows, LANES), 1)
    tile = jnp.zeros((rows, LANES), jnp.float32)
    for k, value in enumerate(values):
        tile = jnp.where(lane == k, value, tile)
    return tile


def diagonal(rows):
    return lax.broadcasted_iota(jnp.int32, (rows, rows), 0) == lax.broadcasted_iota(
        jnp.int32, (rows, rows), 1
    )


def student_kernel(base, labels_hbm, student_hbm, down_hbm, stats, student, down, labels, sems):
    rows, width = student.shape
    parts = spans(width, 4)
    copies = fetched((labels_hbm,), (labels,), sems)
    for k, (start, size) in enumerate(parts):
        part = pl.ds(start, size)
        copy = pltpu.make_async_copy(
            student_hbm.at[:, part], student.at[:, part], sems.at[k + 1]
        )
        copy.start()
        copies.append(copy)
    weight = pltpu.make_async_copy(down_hbm, down, sems.at[len(parts) + 1])
    weight.start()
    copies[0].wait()
    spread_out = jnp.where(diagonal(rows), jnp.broadcast_to(labels[...], (rows, rows)), 0)
    label = jnp.sum(spread_out.astype(jnp.float32), axis=1, keepdims=True).astype(jnp.int32)
    label = label - base[0]
    top = jnp.full((rows, 1), -jnp.inf, jnp.float32)
    for copy, (start, size) in zip(copies[1:], parts):
        copy.wait()
        top = row_max(student, start, size, top)

    def step(at, size):
        value = load(student, at, size)
        here = lax.broadcasted_iota(jnp.int32, (rows, size), 1) == label - at
        return jnp.exp(value - top), jnp.where(here, value, 0.0)

    total, picked = row_sums(width, step)
    zero = jnp.zeros((rows, 1), jnp.float32)
    stats[...] = columns(
        (top, total, picked, zero, zero, zero, label.astype(jnp.float32)), rows
    )
    weight.wait()


def teacher_kernel(student, teacher, student_stats, stats):
    rows, width = student.shape
    top = row_max(teacher, 0, width, jnp.full((rows, 1), -jnp.inf, jnp.float32))

    def step(at, size):
        ours = load(student, at, size)
        theirs = load(teacher, at, size)
        power = jnp.exp(theirs - top)
        return power, power * (theirs - ours)

    total, cross = row_sums(width, step)
    lane = lax.broadcasted_iota(jnp.int32, (rows, LANES), 1)
    tile = student_stats[...]
    tile = jnp.where(lane == 3, top, tile)
    tile = jnp.where(lane == 4, total, tile)
    stats[...] = jnp.where(lane == 5, cross, tile)


def final_kernel(parts, student, teacher, *refs):
    stats, (loss, grad, stage, loss_stage, sems) = refs[:parts], refs[parts:]
    rows, width = student.shape
    tiles = [ref[...] for ref in stats]
    label = tiles[0][:, 6:7].astype(jnp.int32)
    top = functools.reduce(jnp.maximum, tiles)
    smax, tmax = top[:, 0:1], top[:, 3:4]
    ssum = tsum = cross = picked = jnp.zeros((rows, 1), jnp.float32)
    for tile in tiles:
        ssum = ssum + tile[:, 1:2] * jnp.exp(tile[:, 0:1] - smax)
        scale = jnp.exp(tile[:, 3:4] - tmax)
        tsum = tsum + tile[:, 4:5] * scale
        cross = cross + tile[:, 5:6] * scale
        picked = picked + tile[:, 2:3]
    lse_s = smax + jnp.log(ssum)
    lse_t = tmax + jnp.log(tsum)
    value = 2.0 * lse_s - picked + cross / tsum - lse_t
    loss_stage[...] = jnp.sum(jnp.where(diagonal(rows), value, 0.0), axis=0, keepdims=True)
    copies = fetched((loss_stage,), (loss,), sems)
    for k, (start, size) in enumerate(spans(width, 4)):
        for at, span in chunks(start, size):
            here = lax.broadcasted_iota(jnp.int32, (rows, span), 1) == label - at
            result = (
                2.0 * jnp.exp(load(student, at, span) - lse_s)
                - here.astype(jnp.float32)
                - jnp.exp(load(teacher, at, span) - lse_t)
            )
            stage[:, pl.ds(at, span)] = result.astype(jnp.bfloat16)
        part = pl.ds(start, size)
        copy = pltpu.make_async_copy(stage.at[:, part], grad.at[:, part], sems.at[k + 1])
        copy.start()
        copies.append(copy)
    for copy in copies:
        copy.wait()


def distill(student, stale, labels, down_w):
    _, width = student.shape
    teacher = onward(stale, "peer")
    base = (lax.axis_index("grp") * width).astype(jnp.int32).reshape(1)
    own, student, down_w = student_stats(base, labels, student, down_w)
    stats = teacher_stats(student, teacher, own)
    count = lax.axis_size("grp")
    others = []
    for s in range(1, count):
        others.append(
            lax.ppermute(stats, "grp", [(k, (k + s) % count) for k in range(count)])
        )
    loss, grad = finish(student, teacher, [stats, *others])
    return loss, grad, down_w


def student_stats(base, labels, student, down_w):
    rows, width = student.shape
    return pl.pallas_call(
        student_kernel,
        out_shape=(
            jax.ShapeDtypeStruct((rows, LANES), jnp.float32),
            jax.ShapeDtypeStruct(student.shape, student.dtype),
            jax.ShapeDtypeStruct(down_w.shape, down_w.dtype),
        ),
        in_specs=[pl.BlockSpec(memory_space=pltpu.SMEM)] + hbm(3),
        out_specs=tuple(vmem(3)),
        scratch_shapes=[
            pltpu.VMEM(labels.shape, labels.dtype),
            pltpu.SemaphoreType.DMA((len(spans(width, 4)) + 2,)),
        ],
        compiler_params=params(8),
        name="student",
    )(base, *in_hbm(labels, student, down_w))


def teacher_stats(student, teacher, own):
    rows, _ = student.shape
    return pl.pallas_call(
        teacher_kernel,
        out_shape=jax.ShapeDtypeStruct((rows, LANES), jnp.float32),
        in_specs=vmem(3),
        out_specs=vmem(1)[0],
        compiler_params=params(8),
        name="teacher",
    )(student, teacher, own)


def finish(student, teacher, stats):
    rows, width = student.shape
    count = len(stats)
    return pl.pallas_call(
        functools.partial(final_kernel, count),
        out_shape=(
            jax.ShapeDtypeStruct((1, rows), jnp.float32),
            jax.ShapeDtypeStruct((rows, width), jnp.bfloat16),
        ),
        in_specs=vmem(2 + count),
        out_specs=tuple(hbm(2)),
        scratch_shapes=[
            pltpu.VMEM((rows, width), jnp.bfloat16),
            pltpu.VMEM((1, rows), jnp.float32),
            pltpu.SemaphoreType.DMA((len(spans(width, 4)) + 1,)),
        ],
        compiler_params=params(8),
        name="final",
    )(student, teacher, *stats)


def between_blocks(value, n_window):
    if n_window == 1:
        return value
    groups = [[b + PIECES * a for a in range(n_window)] for b in range(PIECES)]
    return lax.all_to_all(
        value, "grp", split_axis=0, concat_axis=0, tiled=True, axis_index_groups=groups
    )


def layer(tokens, cotangent, ids, prob, weights, n_window):
    rows, scaled, slot_cot, select, slot_prob, ids = prepare(ids, prob, tokens, cotangent, n_window)
    rows = between_blocks(rows, n_window)
    scaled = between_blocks(scaled, n_window)
    rows_far = swapped(rows, "grp", 2)
    scaled_far = swapped(scaled, "grp", 2)
    rows_near = swapped(rows, "grp", 1)
    scaled_near = swapped(scaled, "grp", 1)
    rows_cross = swapped(rows_far, "grp", 1)
    scaled_cross = swapped(scaled_far, "grp", 1)

    out_own, out_send, gate, up = forward(rows, rows_near, weights)
    grad_own, grad_send = backward(scaled, scaled_near, gate, up, weights)
    out_back = swapped(out_send, "grp", 1)
    grad_back = swapped(grad_send, "grp", 1)

    out_keep, out_send, gate, up = forward(rows_far, rows_cross, weights)
    out_more = swapped(out_send, "grp", 1)
    grad_keep, grad_send = backward(scaled_far, scaled_cross, gate, up, weights)
    grad_more = swapped(grad_send, "grp", 1)
    out_home = swapped(pair_sum(out_keep, out_more), "grp", 2)
    grad_home = swapped(pair_sum(grad_keep, grad_more), "grp", 2)

    outs = collected([out_own, out_back, out_home], n_window)
    grads = collected([grad_own, grad_back, grad_home], n_window)
    layer_out, prob_grad = combine_out(outs, ids, select, slot_prob, slot_cot, n_window)
    input_grad = combine_grad(grads, select, n_window)
    return layer_out, input_grad, prob_grad


def pair_sum(one, two):
    return (one.astype(jnp.float32) + two.astype(jnp.float32)).astype(jnp.bfloat16)


def collected(parts, n_window):
    if n_window == 1:
        return parts
    total = functools.reduce(jnp.add, [part.astype(jnp.float32) for part in parts])
    return [between_blocks(total.astype(jnp.bfloat16), n_window)]


def body(
    tokens,
    cotangent,
    expert_ids,
    route_prob,
    w_gate,
    w_up,
    w_down,
    student_logits,
    stale_logits,
    labels,
):
    n_window = lax.axis_size("grp") // PIECES
    distill_loss, logit_grad, down_w = distill(
        student_logits[0], stale_logits[0], labels, w_down[0]
    )
    layer_out, input_grad, prob_grad = layer(
        tokens,
        cotangent,
        expert_ids.T,
        route_prob.T,
        (w_gate[0].T, w_up[0].T, down_w),
        n_window,
    )
    return (layer_out, input_grad, prob_grad.T, distill_loss, logit_grad[None])


def solution(mesh):
    placed = (
        P(("peer", "grp"), None),
        P(("peer", "grp"), None),
        P(("peer", "grp"), None),
        P(("peer", "grp"), None),
        P("peer", None, "grp"),
        P("peer", None, "grp"),
        P("peer", "grp", None),
        P("peer", None, "grp"),
        P("peer", None, "grp"),
        P("peer", None),
    )
    return jax.shard_map(
        body,
        mesh=mesh,
        in_specs=placed,
        out_specs=(
            P(("peer", "grp"), None),
            P(("peer", "grp"), None),
            P(("peer", "grp"), None),
            P("peer", None),
            P("peer", None, "grp"),
        ),
        check_vma=False,
    )
```

```python
import functools
import math

import jax
import jax.numpy as jnp
from jax import lax
from jax.experimental import pallas as pl
from jax.experimental.pallas import tpu as pltpu
from jax.sharding import PartitionSpec as P


PIECES = 4
CAP = 32
LANES = 128
CHUNK = 2048
NT = (((1,), (1,)), ((), ()))
TN = (((0,), (0,)), ((), ()))


def vmem(count):
    return [pl.BlockSpec(memory_space=pltpu.VMEM)] * count


def hbm(count):
    return [pl.BlockSpec(memory_space=pltpu.HBM)] * count


def in_hbm(*values):
    return [pltpu.with_memory_space_constraint(value, pltpu.HBM) for value in values]


def params(mib):
    return pltpu.CompilerParams(vmem_limit_bytes=mib * 1024 * 1024)


def swapped(value, axis, bits):
    count = lax.axis_size(axis)
    return lax.ppermute(value, axis, [(k, k ^ bits) for k in range(count)])


def onward(value, axis):
    count = lax.axis_size(axis)
    return lax.ppermute(value, axis, [(k, (k + 1) % count) for k in range(count)])


def fetched(sources, buffers, sems):
    copies = [
        pltpu.make_async_copy(source, buffer, sems.at[k])
        for k, (source, buffer) in enumerate(zip(sources, buffers))
    ]
    for copy in copies:
        copy.start()
    return copies


def prepare_kernel(n_window, held, *refs):
    taken = 4 + held
    sources, refs = refs[:taken], refs[taken:]
    rows, scaled, slot_cot, select, slot_prob, ids = refs[:6]
    kept, (prob, tokens, cot, sems) = refs[6 : 6 + held], refs[6 + held :]
    copies = fetched(sources, (ids, prob, tokens, cot, *kept), sems)
    copies[0].wait()
    copies[1].wait()
    all_ids = ids[...]
    count = all_ids.shape[1]
    before = (
        lax.broadcasted_iota(jnp.int32, (count, count), 0)
        < lax.broadcasted_iota(jnp.int32, (count, count), 1)
    ).astype(jnp.float32).astype(jnp.bfloat16)
    slot = lax.broadcasted_iota(jnp.int32, (CAP, count), 0)
    for e in range(n_window):
        part = pl.ds(e * CAP, CAP)
        hit = all_ids == e
        member = jnp.sum(hit.astype(jnp.float32), axis=0, keepdims=True)
        token_prob = jnp.sum(jnp.where(hit, prob[...], 0.0), axis=0, keepdims=True)
        earlier = jnp.dot(
            jnp.broadcast_to(member, (16, count)).astype(jnp.bfloat16),
            before,
            preferred_element_type=jnp.float32,
        )
        position = earlier[:1].astype(jnp.int32)
        chosen = (slot == position) & (member > 0.5)
        chosen_f = chosen.astype(jnp.float32)
        chosen_b = chosen_f.astype(jnp.bfloat16)
        weight = jnp.sum(chosen_f * token_prob, axis=1, keepdims=True)
        if e == 0:
            copies[2].wait()
        rows[part, :] = jnp.dot(
            chosen_b, tokens[...], preferred_element_type=jnp.float32
        ).astype(jnp.bfloat16)
        if e == 0:
            copies[3].wait()
        cot_rows = jnp.dot(chosen_b, cot[...], preferred_element_type=jnp.float32)
        slot_cot[part, :] = cot_rows.astype(jnp.bfloat16)
        scaled[part, :] = (weight * cot_rows).astype(jnp.bfloat16)
        select[part, :] = chosen_f
        slot_prob[part, :] = jnp.broadcast_to(weight, (CAP, LANES))
    for copy in copies[4:]:
        copy.wait()


def prepare(ids, prob, tokens, cot, held, n_window):
    count, width = tokens.shape
    slots = n_window * CAP
    wide = jax.ShapeDtypeStruct((slots, width), jnp.bfloat16)
    return pl.pallas_call(
        functools.partial(prepare_kernel, n_window, len(held)),
        out_shape=(
            wide,
            wide,
            wide,
            jax.ShapeDtypeStruct((slots, count), jnp.float32),
            jax.ShapeDtypeStruct((slots, LANES), jnp.float32),
            jax.ShapeDtypeStruct(ids.shape, ids.dtype),
            *[jax.ShapeDtypeStruct(value.shape, value.dtype) for value in held],
        ),
        in_specs=hbm(4 + len(held)),
        out_specs=tuple(vmem(6 + len(held))),
        scratch_shapes=[
            pltpu.VMEM(prob.shape, prob.dtype),
            pltpu.VMEM(tokens.shape, tokens.dtype),
            pltpu.VMEM(cot.shape, cot.dtype),
            pltpu.SemaphoreType.DMA((4 + len(held),)),
        ],
        compiler_params=params(8),
        cost_estimate=pl.CostEstimate(flops=20000000000, bytes_accessed=0, transcendentals=0),
        name="prepare",
    )(*in_hbm(ids, prob, tokens, cot, *held))


def forward_math(rows, gate_w, up_w, down_w):
    gate = lax.dot_general(rows, gate_w[...], NT, preferred_element_type=jnp.float32)
    up = lax.dot_general(rows, up_w[...], NT, preferred_element_type=jnp.float32)
    hidden = (gate * jax.nn.sigmoid(gate) * up).astype(jnp.bfloat16)
    out = jnp.dot(hidden, down_w[...], preferred_element_type=jnp.float32)
    return out.astype(jnp.bfloat16), gate, up


def backward_math(scaled, gate, up, gate_w, up_w, down_w):
    sig = jax.nn.sigmoid(gate)
    grad_hidden = lax.dot_general(scaled, down_w[...], NT, preferred_element_type=jnp.float32)
    grad_gate = (grad_hidden * up * sig * (1.0 + gate * (1.0 - sig))).astype(jnp.bfloat16)
    grad_up = (grad_hidden * gate * sig).astype(jnp.bfloat16)
    grad = jnp.dot(grad_gate, gate_w[...], preferred_element_type=jnp.float32)
    grad = grad + jnp.dot(grad_up, up_w[...], preferred_element_type=jnp.float32)
    return grad.astype(jnp.bfloat16)


def forward_kernel(rows_a, rows_b, gate_w, up_w, down_w, keep, send, gate_ref, up_ref):
    half = rows_a.shape[0]
    rows = jnp.concatenate([rows_a[...], rows_b[...]], axis=0)
    out, gate, up = forward_math(rows, gate_w, up_w, down_w)
    keep[...] = out[:half]
    send[...] = out[half:]
    gate_ref[...] = gate
    up_ref[...] = up


def backward_kernel(scaled_a, scaled_b, gate, up, gate_w, up_w, down_w, keep, send):
    half = scaled_a.shape[0]
    scaled = jnp.concatenate([scaled_a[...], scaled_b[...]], axis=0)
    grad = backward_math(scaled, gate[...], up[...], gate_w, up_w, down_w)
    keep[...] = grad[:half]
    send[...] = grad[half:]


def forward(rows_a, rows_b, weights):
    half, width = rows_a.shape
    hidden = weights[0].shape[0]
    part = jax.ShapeDtypeStruct((half, width), jnp.bfloat16)
    act = jax.ShapeDtypeStruct((2 * half, hidden), jnp.float32)
    return pl.pallas_call(
        forward_kernel,
        out_shape=(part, part, act, act),
        in_specs=vmem(5),
        out_specs=tuple(vmem(4)),
        compiler_params=params(12),
        name="forward",
    )(rows_a, rows_b, *weights)


def backward(scaled_a, scaled_b, gate, up, weights):
    half, width = scaled_a.shape
    part = jax.ShapeDtypeStruct((half, width), jnp.bfloat16)
    return pl.pallas_call(
        backward_kernel,
        out_shape=(part, part),
        in_specs=vmem(7),
        out_specs=tuple(vmem(2)),
        compiler_params=params(12),
        name="backward",
    )(scaled_a, scaled_b, gate, up, *weights)


def spread(select, value, exact):
    high = value.astype(jnp.bfloat16)
    chosen = select.astype(jnp.bfloat16)
    total = lax.dot_general(chosen, high, TN, preferred_element_type=jnp.float32)
    if exact:
        return total
    low = (value - high.astype(jnp.float32)).astype(jnp.bfloat16)
    return total + lax.dot_general(chosen, low, TN, preferred_element_type=jnp.float32)


BLOCK = 512


def summed(refs, part):
    total = refs[0][:, part].astype(jnp.float32)
    for other in refs[1:]:
        total = total + other[:, part].astype(jnp.float32)
    return total


def combine_kernel(n_window, parts, *refs):
    outs, grads = refs[:parts], refs[parts : 2 * parts]
    ids, select, slot_prob, slot_cot, layer_out, input_grad, prob_grad = refs[2 * parts : -4]
    out_stage, grad_stage, prob_stage, sems = refs[-4:]
    exact = n_window == 1
    chosen = select[...]
    weight = slot_prob[:, :1]
    width = outs[0].shape[1]
    block = min(BLOCK, width)
    blocks = width // block
    copies = []

    def send(source, target):
        copy = pltpu.make_async_copy(source, target, sems.at[len(copies)])
        copy.start()
        copies.append(copy)

    per_slot = jnp.zeros((chosen.shape[0], 1), jnp.float32)
    for k in range(blocks):
        part = pl.ds(k * block, block)
        out = summed(outs, part)
        per_slot = per_slot + jnp.sum(
            out * slot_cot[:, part].astype(jnp.float32), axis=1, keepdims=True
        )
        out_stage[:, part] = spread(chosen, weight * out, exact).astype(jnp.bfloat16)
        send(out_stage.at[:, part], layer_out.at[:, part])
    spread_prob = chosen * per_slot
    for e in range(n_window):
        per_token = jnp.sum(spread_prob[e * CAP : (e + 1) * CAP], axis=0, keepdims=True)
        kept = jnp.where(ids[...] == e, per_token, 0.0)
        whole = kept if e == 0 else whole + kept
    prob_stage[...] = whole
    send(prob_stage, prob_grad)
    for k in range(blocks):
        part = pl.ds(k * block, block)
        grad_stage[:, part] = spread(chosen, summed(grads, part), exact).astype(jnp.bfloat16)
        send(grad_stage.at[:, part], input_grad.at[:, part])
    for copy in copies:
        copy.wait()


def combine(outs, grads, ids, select, slot_prob, slot_cot, n_window):
    parts = len(outs)
    width = outs[0].shape[1]
    topk, count = ids.shape
    wide = jax.ShapeDtypeStruct((count, width), jnp.bfloat16)
    return pl.pallas_call(
        functools.partial(combine_kernel, n_window, parts),
        out_shape=(wide, wide, jax.ShapeDtypeStruct((topk, count), jnp.float32)),
        in_specs=vmem(2 * parts + 4),
        out_specs=tuple(hbm(3)),
        scratch_shapes=[
            pltpu.VMEM((count, width), jnp.bfloat16),
            pltpu.VMEM((count, width), jnp.bfloat16),
            pltpu.VMEM((topk, count), jnp.float32),
            pltpu.SemaphoreType.DMA((2 * (width // min(BLOCK, width)) + 1,)),
        ],
        compiler_params=params(12),
        name="combine",
    )(*outs, *grads, ids, select, slot_prob, slot_cot)


def spans(width, parts):
    step = CHUNK * max(1, width // (parts * CHUNK))
    return [(start, min(step, width - start)) for start in range(0, width, step)]


def chunks(start, size):
    return [(at, min(CHUNK, start + size - at)) for at in range(start, start + size, CHUNK)]


def load(ref, at, size):
    return ref[:, pl.ds(at, size)].astype(jnp.float32)


def row_max(ref, start, size, top):
    full = None
    for at, span in chunks(start, size):
        value = load(ref, at, span)
        if span < CHUNK:
            top = jnp.maximum(top, jnp.max(value, axis=1, keepdims=True))
        else:
            full = value if full is None else jnp.maximum(full, value)
    if full is not None:
        top = jnp.maximum(top, jnp.max(full, axis=1, keepdims=True))
    return top


def row_sums(width, step):
    full = tail = None
    for at, span in chunks(0, width):
        values = step(at, span)
        if span < CHUNK:
            tail = values
        elif full is None:
            full = values
        else:
            full = tuple(one + two for one, two in zip(full, values))
    sums = [jnp.sum(value, axis=1, keepdims=True) for value in (full or tail)]
    if full is not None and tail is not None:
        more = [jnp.sum(value, axis=1, keepdims=True) for value in tail]
        sums = [one + two for one, two in zip(sums, more)]
    return sums


def columns(values, rows):
    lane = lax.broadcasted_iota(jnp.int32, (rows, LANES), 1)
    tile = jnp.zeros((rows, LANES), jnp.float32)
    for k, value in enumerate(values):
        tile = jnp.where(lane == k, value, tile)
    return tile


def diagonal(rows):
    return lax.broadcasted_iota(jnp.int32, (rows, rows), 0) == lax.broadcasted_iota(
        jnp.int32, (rows, rows), 1
    )


def student_kernel(base, labels, student, stats):
    rows, width = student.shape
    spread_out = jnp.where(diagonal(rows), jnp.broadcast_to(labels[...], (rows, rows)), 0)
    label = jnp.sum(spread_out.astype(jnp.float32), axis=1, keepdims=True).astype(jnp.int32)
    label = label - base[0]
    top = row_max(student, 0, width, jnp.full((rows, 1), -jnp.inf, jnp.float32))

    def step(at, size):
        value = load(student, at, size)
        here = lax.broadcasted_iota(jnp.int32, (rows, size), 1) == label - at
        return jnp.exp(value - top), jnp.where(here, value, 0.0)

    total, picked = row_sums(width, step)
    zero = jnp.zeros((rows, 1), jnp.float32)
    stats[...] = columns(
        (top, total, picked, zero, zero, zero, label.astype(jnp.float32)), rows
    )


def teacher_kernel(student, teacher, student_stats, stats):
    rows, width = student.shape
    top = row_max(teacher, 0, width, jnp.full((rows, 1), -jnp.inf, jnp.float32))

    def step(at, size):
        ours = load(student, at, size)
        theirs = load(teacher, at, size)
        high = jnp.exp(theirs - top)
        return high, high * (theirs - ours)

    total, cross = row_sums(width, step)
    lane = lax.broadcasted_iota(jnp.int32, (rows, LANES), 1)
    tile = student_stats[...]
    tile = jnp.where(lane == 3, top, tile)
    tile = jnp.where(lane == 4, total, tile)
    stats[...] = jnp.where(lane == 5, cross, tile)


def joined(one, two):
    lane = lax.broadcasted_iota(jnp.int32, one.shape, 1)
    student = lane < 2
    top_one = jnp.where(student, one[:, 0:1], one[:, 3:4])
    top_two = jnp.where(student, two[:, 0:1], two[:, 3:4])
    top = jnp.maximum(top_one, top_two)
    scaled = one * jnp.exp(top_one - top) + two * jnp.exp(top_two - top)
    tile = jnp.where((lane == 0) | (lane == 3), top, scaled)
    tile = jnp.where(lane == 2, one + two, tile)
    return jnp.where(lane == 6, one, tile)


def joined_all(tiles):
    while len(tiles) > 1:
        pairs = [joined(*tiles[k : k + 2]) for k in range(0, len(tiles) - 1, 2)]
        tiles = pairs + tiles[2 * len(pairs) :]
    return tiles[0]


def join_kernel(*refs):
    refs[-1][...] = joined_all([ref[...] for ref in refs[:-1]])


def join(tiles):
    return pl.pallas_call(
        join_kernel,
        out_shape=jax.ShapeDtypeStruct(tiles[0].shape, tiles[0].dtype),
        in_specs=vmem(len(tiles)),
        out_specs=vmem(1)[0],
        compiler_params=params(1),
        name="join",
    )(*tiles)


def final_kernel(student, teacher, *refs):
    tiles, (loss, grad, stage, loss_stage, sems) = refs[:-5], refs[-5:]
    rows, width = student.shape
    tile = joined_all([ref[...] for ref in tiles])
    smax, ssum, picked = tile[:, 0:1], tile[:, 1:2], tile[:, 2:3]
    tmax, tsum, cross = tile[:, 3:4], tile[:, 4:5], tile[:, 5:6]
    label = tiles[0][:, 6:7].astype(jnp.int32)
    lse_s = smax + jnp.log(ssum)
    lse_t = tmax + jnp.log(tsum)
    half_s = lse_s - math.log(2.0)
    value = 2.0 * lse_s - picked + cross / tsum - lse_t
    loss_stage[...] = jnp.sum(jnp.where(diagonal(rows), value, 0.0), axis=0, keepdims=True)
    copies = fetched((loss_stage,), (loss,), sems)
    for k, (start, size) in enumerate(spans(width, 20)):
        for at, span in chunks(start, size):
            here = lax.broadcasted_iota(jnp.int32, (rows, span), 1) == label - at
            part = pl.ds(at, span)
            twice = jnp.exp(load(student, at, span) - half_s)
            result = twice - jnp.exp(load(teacher, at, span) - lse_t)
            result = jnp.where(here, result - 1.0, result)
            stage[:, pl.ds(at, span)] = result.astype(jnp.bfloat16)
        part = pl.ds(start, size)
        copy = pltpu.make_async_copy(stage.at[:, part], grad.at[:, part], sems.at[k + 1])
        copy.start()
        copies.append(copy)
    for copy in copies:
        copy.wait()


def distill(student, teacher, labels):
    base = (lax.axis_index("grp") * student.shape[1]).astype(jnp.int32).reshape(1)
    own = student_stats(base, labels, student)
    stats = teacher_stats(student, teacher, own)
    tiles = exchanged(stats, 1)
    bits = 4
    while bits < lax.axis_size("grp"):
        stats = join(tiles)
        tiles = exchanged(stats, bits)
        bits = 4 * bits
    loss, grad = finish(student, teacher, tiles)
    return loss, grad


def exchanged(tile, bits):
    tiles = [tile]
    for k in (1, 2, 3):
        if k * bits < lax.axis_size("grp"):
            tiles.append(swapped(tile, "grp", k * bits))
    return tiles


def student_stats(base, labels, student):
    return pl.pallas_call(
        student_kernel,
        out_shape=jax.ShapeDtypeStruct((student.shape[0], LANES), jnp.float32),
        in_specs=[pl.BlockSpec(memory_space=pltpu.SMEM)] + vmem(2),
        out_specs=vmem(1)[0],
        compiler_params=params(8),
        name="student",
    )(base, labels, student)


def teacher_stats(student, teacher, own):
    rows, _ = student.shape
    return pl.pallas_call(
        teacher_kernel,
        out_shape=jax.ShapeDtypeStruct((rows, LANES), jnp.float32),
        in_specs=vmem(3),
        out_specs=vmem(1)[0],
        compiler_params=params(8),
        name="teacher",
    )(student, teacher, own)


def finish(student, teacher, tiles):
    rows, width = student.shape
    return pl.pallas_call(
        final_kernel,
        out_shape=(
            jax.ShapeDtypeStruct((1, rows), jnp.float32),
            jax.ShapeDtypeStruct((rows, width), jnp.bfloat16),
        ),
        in_specs=vmem(2 + len(tiles)),
        out_specs=tuple(hbm(2)),
        scratch_shapes=[
            pltpu.VMEM((rows, width), jnp.bfloat16),
            pltpu.VMEM((1, rows), jnp.float32),
            pltpu.SemaphoreType.DMA((len(spans(width, 20)) + 1,)),
        ],
        compiler_params=params(8),
        name="final",
    )(student, teacher, *tiles)


def between_blocks(value, n_window):
    if n_window == 1:
        return value
    groups = [[b + PIECES * a for a in range(n_window)] for b in range(PIECES)]
    return lax.all_to_all(
        value, "grp", split_axis=0, concat_axis=0, tiled=True, axis_index_groups=groups
    )


def layer(rows, scaled, slot_cot, select, slot_prob, ids, weights, n_window):
    rows = between_blocks(rows, n_window)
    scaled = between_blocks(scaled, n_window)
    rows_far = swapped(rows, "grp", 2)
    scaled_far = swapped(scaled, "grp", 2)
    rows_near = swapped(rows, "grp", 1)
    scaled_near = swapped(scaled, "grp", 1)
    rows_cross = swapped(rows_far, "grp", 1)
    scaled_cross = swapped(scaled_far, "grp", 1)

    out_own, out_send, gate, up = forward(rows, rows_near, weights)
    grad_own, grad_send = backward(scaled, scaled_near, gate, up, weights)
    out_back = swapped(out_send, "grp", 1)
    grad_back = swapped(grad_send, "grp", 1)

    out_keep, out_send, gate, up = forward(rows_far, rows_cross, weights)
    out_more = swapped(out_send, "grp", 1)
    grad_keep, grad_send = backward(scaled_far, scaled_cross, gate, up, weights)
    grad_more = swapped(grad_send, "grp", 1)
    out_home = swapped(pair_sum(out_keep, out_more), "grp", 2)
    grad_home = swapped(pair_sum(grad_keep, grad_more), "grp", 2)

    outs = collected([out_own, out_back, out_home], n_window)
    grads = collected([grad_own, grad_back, grad_home], n_window)
    return combine(outs, grads, ids, select, slot_prob, slot_cot, n_window)


def pair_sum(one, two):
    return (one.astype(jnp.float32) + two.astype(jnp.float32)).astype(jnp.bfloat16)


def collected(parts, n_window):
    if n_window == 1:
        return parts
    total = functools.reduce(jnp.add, [part.astype(jnp.float32) for part in parts])
    return [between_blocks(total.astype(jnp.bfloat16), n_window)]


def body(
    tokens,
    cotangent,
    expert_ids,
    route_prob,
    w_gate,
    w_up,
    w_down,
    student_logits,
    stale_logits,
    labels,
):
    n_window = lax.axis_size("grp") // PIECES
    teacher = onward(stale_logits[0], "peer")
    held = (labels,)
    *slots, labels = prepare(
        expert_ids.T, route_prob.T, tokens, cotangent, held, n_window
    )
    gate_w, up_w, down_w, student = (w_gate[0].T, w_up[0].T, w_down[0], student_logits[0])
    layer_out, input_grad, prob_grad = layer(*slots, (gate_w, up_w, down_w), n_window)
    distill_loss, logit_grad = distill(student, teacher, labels)
    return (layer_out, input_grad, prob_grad.T, distill_loss, logit_grad[None])


def solution(mesh):
    placed = (
        P(("peer", "grp"), None),
        P(("peer", "grp"), None),
        P(("peer", "grp"), None),
        P(("peer", "grp"), None),
        P("peer", None, "grp"),
        P("peer", None, "grp"),
        P("peer", "grp", None),
        P("peer", None, "grp"),
        P("peer", None, "grp"),
        P("peer", None),
    )
    return jax.shard_map(
        body,
        mesh=mesh,
        in_specs=placed,
        out_specs=(
            P(("peer", "grp"), None),
            P(("peer", "grp"), None),
            P(("peer", "grp"), None),
            P("peer", None),
            P("peer", None, "grp"),
        ),
        check_vma=False,
    )
```

```python
import functools

import jax
import jax.numpy as jnp
from jax import lax
from jax.experimental import pallas as pl
from jax.experimental.pallas import tpu as pltpu
from jax.sharding import PartitionSpec as P


PIECES = 4
CAP = 32
LANES = 128
CHUNK = 2048
NT = (((1,), (1,)), ((), ()))
TN = (((0,), (0,)), ((), ()))


def vmem(count):
    return [pl.BlockSpec(memory_space=pltpu.VMEM)] * count


def hbm(count):
    return [pl.BlockSpec(memory_space=pltpu.HBM)] * count


def in_hbm(*values):
    return [pltpu.with_memory_space_constraint(value, pltpu.HBM) for value in values]


def params(mib):
    return pltpu.CompilerParams(vmem_limit_bytes=mib * 1024 * 1024)


def swapped(value, axis, bits):
    count = lax.axis_size(axis)
    return lax.ppermute(value, axis, [(k, k ^ bits) for k in range(count)])


def onward(value, axis):
    count = lax.axis_size(axis)
    return lax.ppermute(value, axis, [(k, (k + 1) % count) for k in range(count)])


def fetched(sources, buffers, sems):
    copies = [
        pltpu.make_async_copy(source, buffer, sems.at[k])
        for k, (source, buffer) in enumerate(zip(sources, buffers))
    ]
    for copy in copies:
        copy.start()
    return copies


def prepare_kernel(n_window, held, *refs):
    taken = 4 + held
    sources, refs = refs[:taken], refs[taken:]
    rows, scaled, slot_cot, select, slot_prob, ids = refs[:6]
    kept, (prob, tokens, cot, sems) = refs[6 : 6 + held], refs[6 + held :]
    copies = fetched(sources, (ids, prob, tokens, cot, *kept), sems)
    copies[0].wait()
    copies[1].wait()
    all_ids = ids[...]
    count = all_ids.shape[1]
    before = (
        lax.broadcasted_iota(jnp.int32, (count, count), 0)
        < lax.broadcasted_iota(jnp.int32, (count, count), 1)
    ).astype(jnp.float32).astype(jnp.bfloat16)
    slot = lax.broadcasted_iota(jnp.int32, (CAP, count), 0)
    for e in range(n_window):
        part = pl.ds(e * CAP, CAP)
        hit = all_ids == e
        member = jnp.sum(hit.astype(jnp.float32), axis=0, keepdims=True)
        token_prob = jnp.sum(jnp.where(hit, prob[...], 0.0), axis=0, keepdims=True)
        earlier = jnp.dot(
            jnp.broadcast_to(member, (16, count)).astype(jnp.bfloat16),
            before,
            preferred_element_type=jnp.float32,
        )
        position = earlier[:1].astype(jnp.int32)
        chosen = (slot == position) & (member > 0.5)
        chosen_f = chosen.astype(jnp.float32)
        chosen_b = chosen_f.astype(jnp.bfloat16)
        weight = jnp.sum(chosen_f * token_prob, axis=1, keepdims=True)
        if e == 0:
            copies[2].wait()
        rows[part, :] = jnp.dot(
            chosen_b, tokens[...], preferred_element_type=jnp.float32
        ).astype(jnp.bfloat16)
        if e == 0:
            copies[3].wait()
        cot_rows = jnp.dot(chosen_b, cot[...], preferred_element_type=jnp.float32)
        slot_cot[part, :] = cot_rows.astype(jnp.bfloat16)
        scaled[part, :] = (weight * cot_rows).astype(jnp.bfloat16)
        select[part, :] = chosen_f
        slot_prob[part, :] = jnp.broadcast_to(weight, (CAP, LANES))
    for copy in copies[4:]:
        copy.wait()


def prepare(ids, prob, tokens, cot, held, n_window):
    count, width = tokens.shape
    slots = n_window * CAP
    wide = jax.ShapeDtypeStruct((slots, width), jnp.bfloat16)
    return pl.pallas_call(
        functools.partial(prepare_kernel, n_window, len(held)),
        out_shape=(
            wide,
            wide,
            wide,
            jax.ShapeDtypeStruct((slots, count), jnp.float32),
            jax.ShapeDtypeStruct((slots, LANES), jnp.float32),
            jax.ShapeDtypeStruct(ids.shape, ids.dtype),
            *[jax.ShapeDtypeStruct(value.shape, value.dtype) for value in held],
        ),
        in_specs=hbm(4 + len(held)),
        out_specs=tuple(vmem(6 + len(held))),
        scratch_shapes=[
            pltpu.VMEM(prob.shape, prob.dtype),
            pltpu.VMEM(tokens.shape, tokens.dtype),
            pltpu.VMEM(cot.shape, cot.dtype),
            pltpu.SemaphoreType.DMA((4 + len(held),)),
        ],
        compiler_params=params(8),
        cost_estimate=pl.CostEstimate(flops=20000000000, bytes_accessed=0, transcendentals=0),
        name="prepare",
    )(*in_hbm(ids, prob, tokens, cot, *held))


def forward_math(rows, gate_w, up_w, down_w):
    gate = lax.dot_general(rows, gate_w[...], NT, preferred_element_type=jnp.float32)
    up = lax.dot_general(rows, up_w[...], NT, preferred_element_type=jnp.float32)
    hidden = (gate * jax.nn.sigmoid(gate) * up).astype(jnp.bfloat16)
    out = jnp.dot(hidden, down_w[...], preferred_element_type=jnp.float32)
    return out.astype(jnp.bfloat16), gate, up


def backward_math(scaled, gate, up, gate_w, up_w, down_w):
    sig = jax.nn.sigmoid(gate)
    grad_hidden = lax.dot_general(scaled, down_w[...], NT, preferred_element_type=jnp.float32)
    grad_gate = (grad_hidden * up * sig * (1.0 + gate * (1.0 - sig))).astype(jnp.bfloat16)
    grad_up = (grad_hidden * gate * sig).astype(jnp.bfloat16)
    grad = jnp.dot(grad_gate, gate_w[...], preferred_element_type=jnp.float32)
    grad = grad + jnp.dot(grad_up, up_w[...], preferred_element_type=jnp.float32)
    return grad.astype(jnp.bfloat16)


def forward_kernel(rows_a, rows_b, gate_w, up_w, down_w, keep, send, gate_ref, up_ref):
    half = rows_a.shape[0]
    rows = jnp.concatenate([rows_a[...], rows_b[...]], axis=0)
    out, gate, up = forward_math(rows, gate_w, up_w, down_w)
    keep[...] = out[:half]
    send[...] = out[half:]
    gate_ref[...] = gate
    up_ref[...] = up


def backward_kernel(scaled_a, scaled_b, gate, up, gate_w, up_w, down_w, keep, send):
    half = scaled_a.shape[0]
    scaled = jnp.concatenate([scaled_a[...], scaled_b[...]], axis=0)
    grad = backward_math(scaled, gate[...], up[...], gate_w, up_w, down_w)
    keep[...] = grad[:half]
    send[...] = grad[half:]


def forward(rows_a, rows_b, weights):
    half, width = rows_a.shape
    hidden = weights[0].shape[0]
    part = jax.ShapeDtypeStruct((half, width), jnp.bfloat16)
    act = jax.ShapeDtypeStruct((2 * half, hidden), jnp.float32)
    return pl.pallas_call(
        forward_kernel,
        out_shape=(part, part, act, act),
        in_specs=vmem(5),
        out_specs=tuple(vmem(4)),
        compiler_params=params(12),
        name="forward",
    )(rows_a, rows_b, *weights)


def backward(scaled_a, scaled_b, gate, up, weights):
    half, width = scaled_a.shape
    part = jax.ShapeDtypeStruct((half, width), jnp.bfloat16)
    return pl.pallas_call(
        backward_kernel,
        out_shape=(part, part),
        in_specs=vmem(7),
        out_specs=tuple(vmem(2)),
        compiler_params=params(12),
        name="backward",
    )(scaled_a, scaled_b, gate, up, *weights)


def spread(select, value, exact):
    high = value.astype(jnp.bfloat16)
    chosen = select.astype(jnp.bfloat16)
    total = lax.dot_general(chosen, high, TN, preferred_element_type=jnp.float32)
    if exact:
        return total
    low = (value - high.astype(jnp.float32)).astype(jnp.bfloat16)
    return total + lax.dot_general(chosen, low, TN, preferred_element_type=jnp.float32)


BLOCK = 512


def summed(refs, part):
    total = refs[0][:, part].astype(jnp.float32)
    for other in refs[1:]:
        total = total + other[:, part].astype(jnp.float32)
    return total


def combine_kernel(n_window, parts, *refs):
    outs = refs[:parts]
    ids, select, slot_prob, slot_cot, layer_out, prob_grad, stage, prob_stage, sems = refs[parts:]
    exact = n_window == 1
    chosen = select[...]
    weight = slot_prob[:, :1]
    width = outs[0].shape[1]
    block = min(BLOCK, width)
    copies = []

    def send(source, target):
        copy = pltpu.make_async_copy(source, target, sems.at[len(copies)])
        copy.start()
        copies.append(copy)

    per_slot = jnp.zeros((chosen.shape[0], 1), jnp.float32)
    for k in range(width // block):
        part = pl.ds(k * block, block)
        out = summed(outs, part)
        per_slot = per_slot + jnp.sum(
            out * slot_cot[:, part].astype(jnp.float32), axis=1, keepdims=True
        )
        stage[:, part] = spread(chosen, weight * out, exact).astype(jnp.bfloat16)
        send(stage.at[:, part], layer_out.at[:, part])
    spread_prob = chosen * per_slot
    for e in range(n_window):
        per_token = jnp.sum(spread_prob[e * CAP : (e + 1) * CAP], axis=0, keepdims=True)
        kept = jnp.where(ids[...] == e, per_token, 0.0)
        whole = kept if e == 0 else whole + kept
    prob_stage[...] = whole
    send(prob_stage, prob_grad)
    for copy in copies:
        copy.wait()


def combine(outs, ids, select, slot_prob, slot_cot, n_window):
    parts = len(outs)
    width = outs[0].shape[1]
    topk, count = ids.shape
    return pl.pallas_call(
        functools.partial(combine_kernel, n_window, parts),
        out_shape=(
            jax.ShapeDtypeStruct((count, width), jnp.bfloat16),
            jax.ShapeDtypeStruct((topk, count), jnp.float32),
        ),
        in_specs=vmem(parts + 4),
        out_specs=tuple(hbm(2)),
        scratch_shapes=[
            pltpu.VMEM((count, width), jnp.bfloat16),
            pltpu.VMEM((topk, count), jnp.float32),
            pltpu.SemaphoreType.DMA((width // min(BLOCK, width) + 1,)),
        ],
        compiler_params=params(12),
        name="combine",
    )(*outs, ids, select, slot_prob, slot_cot)


def chunks(start, size):
    return [(at, min(CHUNK, start + size - at)) for at in range(start, start + size, CHUNK)]


def load(ref, at, size):
    return ref[:, pl.ds(at, size)].astype(jnp.float32)


def row_max(ref, width):
    full, tail = None, None
    for at, span in chunks(0, width):
        value = ref[:, pl.ds(at, span)]
        if span < CHUNK:
            tail = value
        else:
            full = value if full is None else jnp.maximum(full, value)
    tops = [
        jnp.max(value.astype(jnp.float32), axis=1, keepdims=True)
        for value in (full, tail)
        if value is not None
    ]
    return functools.reduce(jnp.maximum, tops)


def row_sums(width, step):
    full = tail = None
    for at, span in chunks(0, width):
        values = step(at, span)
        if span < CHUNK:
            tail = values
        elif full is None:
            full = values
        else:
            full = tuple(one + two for one, two in zip(full, values))
    sums = [jnp.sum(value, axis=1, keepdims=True) for value in (full or tail)]
    if full is not None and tail is not None:
        more = [jnp.sum(value, axis=1, keepdims=True) for value in tail]
        sums = [one + two for one, two in zip(sums, more)]
    return sums


def columns(values, rows):
    lane = lax.broadcasted_iota(jnp.int32, (rows, LANES), 1)
    tile = jnp.zeros((rows, LANES), jnp.float32)
    for k, value in enumerate(values):
        tile = jnp.where(lane == k, value, tile)
    return tile


def diagonal(rows):
    return lax.broadcasted_iota(jnp.int32, (rows, rows), 0) == lax.broadcasted_iota(
        jnp.int32, (rows, rows), 1
    )


def student_kernel(base, labels, student, stats, power, hit):
    rows, width = student.shape
    spread_out = jnp.where(diagonal(rows), jnp.broadcast_to(labels[...], (rows, rows)), 0)
    label = jnp.sum(spread_out.astype(jnp.float32), axis=1, keepdims=True).astype(jnp.int32)
    label = label - base[0]
    top = row_max(student, width)

    def step(at, size):
        value = load(student, at, size)
        here = lax.broadcasted_iota(jnp.int32, (rows, size), 1) == label - at
        high = jnp.exp(value - top)
        power[:, pl.ds(at, size)] = high
        hit[:, pl.ds(at, size)] = here.astype(jnp.float32)
        return high, jnp.where(here, value, 0.0)

    total, picked = row_sums(width, step)
    zero = jnp.zeros((rows, 1), jnp.float32)
    stats[:rows, :] = columns((top,), rows)
    stats[rows:, :] = columns((total, zero, zero, picked), rows)


def lanes_of(value):
    return [value[:, k : k + LANES] for k in range(0, value.shape[1], LANES)]


def added(values):
    while len(values) > 1:
        pairs = [one + two for one, two in zip(values[::2], values[1::2])]
        values = pairs + values[2 * len(pairs) :]
    return values[0]


def teacher_kernel(student, teacher, student_stats, stats):
    rows, width = student.shape
    top = None
    for at, span in chunks(0, width):
        ours, theirs = lanes_of(load(student, at, span)), lanes_of(load(teacher, at, span))
        ragged = span % LANES
        if ragged:
            pad = jnp.full((rows, LANES - ragged), -jnp.inf, jnp.float32)
            theirs[-1] = jnp.concatenate([theirs[-1], pad], axis=1)
            ours[-1] = jnp.concatenate([ours[-1], jnp.zeros_like(pad)], axis=1)
        high = functools.reduce(jnp.maximum, theirs)
        if top is None:
            total = cross = jnp.zeros((rows, LANES), jnp.float32)
        else:
            high = jnp.maximum(top, high)
            shrink = jnp.exp(top - high)
            total, cross = total * shrink, cross * shrink
        top = high
        powers = [jnp.exp(their - top) for their in theirs]
        gaps = [their - our for our, their in zip(ours, theirs)]
        if ragged:
            gaps[-1] = jnp.where(powers[-1] > 0.0, gaps[-1], 0.0)
        total = total + added(powers)
        cross = cross + added([power * gap for power, gap in zip(powers, gaps)])
    high = jnp.max(top, axis=1, keepdims=True)
    shrink = jnp.exp(top - high)
    total = jnp.sum(total * shrink, axis=1, keepdims=True)
    cross = jnp.sum(cross * shrink, axis=1, keepdims=True)
    top = high
    lane = lax.broadcasted_iota(jnp.int32, (rows, LANES), 1)
    theirs = (lane == 1) | (lane == 2)
    stats[:rows, :] = jnp.where(theirs, top, student_stats[:rows, :])
    value = jnp.where(lane == 1, total, student_stats[rows:, :])
    stats[rows:, :] = jnp.where(lane == 2, cross, value)


def power_kernel(teacher, stats, power):
    top = stats[: teacher.shape[0], 1:2]
    for at, span in chunks(0, teacher.shape[1]):
        power[:, pl.ds(at, span)] = jnp.exp(load(teacher, at, span) - top)


def teacher_power(teacher, stats):
    return pl.pallas_call(
        power_kernel,
        out_shape=jax.ShapeDtypeStruct(teacher.shape, jnp.float32),
        in_specs=vmem(2),
        out_specs=vmem(1)[0],
        compiler_params=params(8),
        name="power",
    )(teacher, stats)


def joined(tiles):
    rows = tiles[0].shape[0] // 2
    tops = [tile[:rows, :] for tile in tiles]
    top = functools.reduce(jnp.maximum, tops)
    parts = [tile[rows:, :] * jnp.exp(one - top) for tile, one in zip(tiles, tops)]
    return top, functools.reduce(jnp.add, parts)


def join_kernel(*refs):
    tiles, out = refs[:-1], refs[-1]
    rows = out.shape[0] // 2
    top, value = joined(tiles)
    out[:rows, :] = top
    out[rows:, :] = value


def join(tiles):
    return pl.pallas_call(
        join_kernel,
        out_shape=jax.ShapeDtypeStruct(tiles[0].shape, tiles[0].dtype),
        in_specs=vmem(len(tiles)),
        out_specs=vmem(1)[0],
        compiler_params=params(1),
        name="join",
    )(*tiles)


def final_kernel(n_window, parts, student, teacher, hit, own, *refs):
    grads, select = refs[:parts], refs[parts]
    loss, logit_grad, input_grad, logit_stage, input_stage, loss_stage, sems = refs[-7:]
    tiles = refs[parts + 1 : -7]
    rows, width = student.shape
    chosen = select[...]
    model_width = grads[0].shape[1]
    block = min(BLOCK, model_width)
    for k in range(model_width // block):
        part = pl.ds(k * block, block)
        value = spread(chosen, summed(grads, part), n_window == 1)
        input_stage[:, part] = value.astype(jnp.bfloat16)
    input_copy = pltpu.make_async_copy(input_stage, input_grad, sems.at[2])
    input_copy.start()
    top, value = joined(tiles)
    lse = top + jnp.log(value)
    scale = jnp.exp(own[:rows, :] - lse)
    scale_s = 2.0 * scale[:, 0:1]
    scale_t = scale[:, 1:2]
    for at, span in chunks(0, width):
        part = pl.ds(at, span)
        result = student[:, part] * scale_s - teacher[:, part] * scale_t - hit[:, part]
        logit_stage[:, part] = result.astype(jnp.bfloat16)
    logit_copy = pltpu.make_async_copy(logit_stage, logit_grad, sems.at[0])
    logit_copy.start()
    picked, cross = value[:, 3:4], value[:, 2:3]
    total = 2.0 * lse[:, 0:1] - picked + cross / value[:, 1:2] - lse[:, 1:2]
    loss_stage[...] = jnp.sum(jnp.where(diagonal(rows), total, 0.0), axis=0, keepdims=True)
    loss_copy = pltpu.make_async_copy(loss_stage, loss, sems.at[1])
    loss_copy.start()
    input_copy.wait()
    logit_copy.wait()
    loss_copy.wait()


def distill(student, teacher, labels):
    base = (lax.axis_index("grp") * student.shape[1]).astype(jnp.int32).reshape(1)
    own, power_s, hit = student_stats(base, labels, student)
    stats = teacher_stats(student, teacher, own)
    first = stats
    tiles = exchanged(stats, 1)
    power_t = teacher_power(teacher, stats)
    bits = 4
    while bits < lax.axis_size("grp"):
        stats = join(tiles)
        tiles = exchanged(stats, bits)
        bits = 4 * bits
    return (power_s, power_t, hit, first), tiles


def exchanged(tile, bits):
    tiles = [tile]
    for k in (1, 2, 3):
        if k * bits < lax.axis_size("grp"):
            tiles.append(swapped(tile, "grp", k * bits))
    return tiles


def student_stats(base, labels, student):
    return pl.pallas_call(
        student_kernel,
        out_shape=(
            jax.ShapeDtypeStruct((2 * student.shape[0], LANES), jnp.float32),
            jax.ShapeDtypeStruct(student.shape, jnp.float32),
            jax.ShapeDtypeStruct(student.shape, jnp.float32),
        ),
        in_specs=[pl.BlockSpec(memory_space=pltpu.SMEM)] + vmem(2),
        out_specs=tuple(vmem(3)),
        compiler_params=params(8),
        name="student",
    )(base, labels, student)


def teacher_stats(student, teacher, own):
    rows, _ = student.shape
    return pl.pallas_call(
        teacher_kernel,
        out_shape=jax.ShapeDtypeStruct((2 * rows, LANES), jnp.float32),
        in_specs=vmem(3),
        out_specs=vmem(1)[0],
        compiler_params=params(8),
        name="teacher",
    )(student, teacher, own)


def finish(kept, tiles, grads, select, n_window):
    student = kept[0]
    rows = student.shape[0]
    wide = (select.shape[1], grads[0].shape[1])
    return pl.pallas_call(
        functools.partial(final_kernel, n_window, len(grads)),
        out_shape=(
            jax.ShapeDtypeStruct((1, rows), jnp.float32),
            jax.ShapeDtypeStruct(student.shape, jnp.bfloat16),
            jax.ShapeDtypeStruct(wide, jnp.bfloat16),
        ),
        in_specs=vmem(len(kept) + len(grads) + 1 + len(tiles)),
        out_specs=tuple(hbm(3)),
        scratch_shapes=[
            pltpu.VMEM(student.shape, jnp.bfloat16),
            pltpu.VMEM(wide, jnp.bfloat16),
            pltpu.VMEM((1, rows), jnp.float32),
            pltpu.SemaphoreType.DMA((3,)),
        ],
        compiler_params=params(8),
        name="final",
    )(*kept, *grads, select, *tiles)


def between_blocks(value, n_window):
    if n_window == 1:
        return value
    groups = [[b + PIECES * a for a in range(n_window)] for b in range(PIECES)]
    return lax.all_to_all(
        value, "grp", split_axis=0, concat_axis=0, tiled=True, axis_index_groups=groups
    )


def layer(rows, scaled, slot_cot, select, slot_prob, ids, weights, n_window):
    rows = between_blocks(rows, n_window)
    scaled = between_blocks(scaled, n_window)
    rows_far = swapped(rows, "grp", 2)
    scaled_far = swapped(scaled, "grp", 2)
    rows_near = swapped(rows, "grp", 1)
    scaled_near = swapped(scaled, "grp", 1)
    rows_cross = swapped(rows_far, "grp", 1)
    scaled_cross = swapped(scaled_far, "grp", 1)

    out_own, out_send, gate, up = forward(rows, rows_near, weights)
    grad_own, grad_send = backward(scaled, scaled_near, gate, up, weights)
    out_back = swapped(out_send, "grp", 1)
    grad_back = swapped(grad_send, "grp", 1)

    out_keep, out_send, gate, up = forward(rows_far, rows_cross, weights)
    out_more = swapped(out_send, "grp", 1)
    grad_keep, grad_send = backward(scaled_far, scaled_cross, gate, up, weights)
    grad_more = swapped(grad_send, "grp", 1)
    out_home = swapped(pair_sum(out_keep, out_more), "grp", 2)
    grad_home = swapped(pair_sum(grad_keep, grad_more), "grp", 2)

    outs = collected([out_own, out_back, out_home], n_window)
    grads = collected([grad_own, grad_back, grad_home], n_window)
    layer_out, prob_grad = combine(outs, ids, select, slot_prob, slot_cot, n_window)
    return layer_out, prob_grad, grads, select


def pair_sum(one, two):
    return (one.astype(jnp.float32) + two.astype(jnp.float32)).astype(jnp.bfloat16)


def collected(parts, n_window):
    if n_window == 1:
        return parts
    total = functools.reduce(jnp.add, [part.astype(jnp.float32) for part in parts])
    return [between_blocks(total.astype(jnp.bfloat16), n_window)]


def body(
    tokens,
    cotangent,
    expert_ids,
    route_prob,
    w_gate,
    w_up,
    w_down,
    student_logits,
    stale_logits,
    labels,
):
    n_window = lax.axis_size("grp") // PIECES
    teacher = onward(stale_logits[0], "peer")
    held = (labels,)
    *slots, labels = prepare(
        expert_ids.T, route_prob.T, tokens, cotangent, held, n_window
    )
    gate_w, up_w, down_w, student = (w_gate[0].T, w_up[0].T, w_down[0], student_logits[0])
    layer_out, prob_grad, grads, select = layer(*slots, (gate_w, up_w, down_w), n_window)
    kept, tiles = distill(student, teacher, labels)
    distill_loss, logit_grad, input_grad = finish(kept, tiles, grads, select, n_window)
    return (layer_out, input_grad, prob_grad.T, distill_loss, logit_grad[None])


def solution(mesh):
    placed = (
        P(("peer", "grp"), None),
        P(("peer", "grp"), None),
        P(("peer", "grp"), None),
        P(("peer", "grp"), None),
        P("peer", None, "grp"),
        P("peer", None, "grp"),
        P("peer", "grp", None),
        P("peer", None, "grp"),
        P("peer", None, "grp"),
        P("peer", None),
    )
    return jax.shard_map(
        body,
        mesh=mesh,
        in_specs=placed,
        out_specs=(
            P(("peer", "grp"), None),
            P(("peer", "grp"), None),
            P(("peer", "grp"), None),
            P("peer", None),
            P("peer", None, "grp"),
        ),
        check_vma=False,
    )
```

```python
import functools

import jax
import jax.numpy as jnp
from jax import lax
from jax.experimental import pallas as pl
from jax.experimental.pallas import tpu as pltpu
from jax.sharding import PartitionSpec as P


PIECES = 4
CAP = 32
LANES = 128
CHUNK = 2048
NT = (((1,), (1,)), ((), ()))
TN = (((0,), (0,)), ((), ()))


def vmem(count):
    return [pl.BlockSpec(memory_space=pltpu.VMEM)] * count


def hbm(count):
    return [pl.BlockSpec(memory_space=pltpu.HBM)] * count


def in_hbm(*values):
    return [pltpu.with_memory_space_constraint(value, pltpu.HBM) for value in values]


def params(mib):
    return pltpu.CompilerParams(vmem_limit_bytes=mib * 1024 * 1024)


def swapped(value, axis, bits):
    count = lax.axis_size(axis)
    return lax.ppermute(value, axis, [(k, k ^ bits) for k in range(count)])


def onward(value, axis):
    count = lax.axis_size(axis)
    return lax.ppermute(value, axis, [(k, (k + 1) % count) for k in range(count)])


def fetched(sources, buffers, sems):
    copies = [
        pltpu.make_async_copy(source, buffer, sems.at[k])
        for k, (source, buffer) in enumerate(zip(sources, buffers))
    ]
    for copy in copies:
        copy.start()
    return copies


def rows_kernel(n_window, ids_hbm, tokens_hbm, rows, select, ids, tokens, sems):
    copies = fetched((ids_hbm, tokens_hbm), (ids, tokens), sems)
    copies[0].wait()
    all_ids = ids[...]
    count = all_ids.shape[1]
    before = (
        lax.broadcasted_iota(jnp.int32, (count, count), 0)
        < lax.broadcasted_iota(jnp.int32, (count, count), 1)
    ).astype(jnp.float32).astype(jnp.bfloat16)
    slot = lax.broadcasted_iota(jnp.int32, (CAP, count), 0)
    for e in range(n_window):
        part = pl.ds(e * CAP, CAP)
        hit = all_ids == e
        member = jnp.sum(hit.astype(jnp.float32), axis=0, keepdims=True)
        earlier = jnp.dot(
            jnp.broadcast_to(member, (16, count)).astype(jnp.bfloat16),
            before,
            preferred_element_type=jnp.float32,
        )
        position = earlier[:1].astype(jnp.int32)
        chosen = ((slot == position) & (member > 0.5)).astype(jnp.float32)
        select[part, :] = chosen
        if e == 0:
            copies[1].wait()
        rows[part, :] = jnp.dot(
            chosen.astype(jnp.bfloat16), tokens[...], preferred_element_type=jnp.float32
        ).astype(jnp.bfloat16)


def scaled_kernel(n_window, ids, select, prob_hbm, cot_hbm, labels_hbm, *refs):
    scaled, slot_cot, slot_prob, labels, prob, cot, sems = refs
    copies = fetched((prob_hbm, cot_hbm, labels_hbm), (prob, cot, labels), sems)
    copies[0].wait()
    for e in range(n_window):
        part = pl.ds(e * CAP, CAP)
        hit = ids[...] == e
        token_prob = jnp.sum(jnp.where(hit, prob[...], 0.0), axis=0, keepdims=True)
        chosen = select[part, :]
        weight = jnp.sum(chosen * token_prob, axis=1, keepdims=True)
        slot_prob[part, :] = jnp.broadcast_to(weight, (CAP, LANES))
        if e == 0:
            copies[1].wait()
        cot_rows = jnp.dot(
            chosen.astype(jnp.bfloat16), cot[...], preferred_element_type=jnp.float32
        )
        slot_cot[part, :] = cot_rows.astype(jnp.bfloat16)
        scaled[part, :] = (weight * cot_rows).astype(jnp.bfloat16)
    copies[2].wait()


def slot_rows(ids, tokens, n_window):
    count, width = tokens.shape
    slots = n_window * CAP
    return pl.pallas_call(
        functools.partial(rows_kernel, n_window),
        out_shape=(
            jax.ShapeDtypeStruct((slots, width), jnp.bfloat16),
            jax.ShapeDtypeStruct((slots, count), jnp.float32),
            jax.ShapeDtypeStruct(ids.shape, ids.dtype),
        ),
        in_specs=hbm(2),
        out_specs=tuple(vmem(3)),
        scratch_shapes=[
            pltpu.VMEM(tokens.shape, tokens.dtype),
            pltpu.SemaphoreType.DMA((2,)),
        ],
        compiler_params=params(8),
        name="slot_rows",
    )(*in_hbm(ids, tokens))


def slot_scaled(ids, select, prob, cot, labels, n_window):
    slots, width = select.shape[0], cot.shape[1]
    wide = jax.ShapeDtypeStruct((slots, width), jnp.bfloat16)
    return pl.pallas_call(
        functools.partial(scaled_kernel, n_window),
        out_shape=(
            wide,
            wide,
            jax.ShapeDtypeStruct((slots, LANES), jnp.float32),
            jax.ShapeDtypeStruct(labels.shape, labels.dtype),
        ),
        in_specs=vmem(2) + hbm(3),
        out_specs=tuple(vmem(4)),
        scratch_shapes=[
            pltpu.VMEM(prob.shape, prob.dtype),
            pltpu.VMEM(cot.shape, cot.dtype),
            pltpu.SemaphoreType.DMA((3,)),
        ],
        compiler_params=params(8),
        name="slot_scaled",
    )(ids, select, *in_hbm(prob, cot, labels))


def forward_half(rows, gate_w, up_w, down_w, act, wait):
    wait(0)
    gate = lax.dot_general(rows, gate_w[...], NT, preferred_element_type=jnp.float32)
    wait(1)
    up = lax.dot_general(rows, up_w[...], NT, preferred_element_type=jnp.float32)
    act[0] = gate
    act[1] = up
    hidden = (gate * jax.nn.sigmoid(gate) * up).astype(jnp.bfloat16)
    wait(2)
    return jnp.dot(hidden, down_w[...], preferred_element_type=jnp.float32)


def backward_half(scaled, act, gate_w, up_w, down_w, wait):
    gate, up = act[0], act[1]
    sig = jax.nn.sigmoid(gate)
    wait(2)
    grad_hidden = lax.dot_general(scaled, down_w[...], NT, preferred_element_type=jnp.float32)
    grad_gate = (grad_hidden * up * sig * (1.0 + gate * (1.0 - sig))).astype(jnp.bfloat16)
    grad_up = (grad_hidden * gate * sig).astype(jnp.bfloat16)
    wait(0)
    grad = jnp.dot(grad_gate, gate_w[...], preferred_element_type=jnp.float32)
    wait(1)
    return grad + jnp.dot(grad_up, up_w[...], preferred_element_type=jnp.float32)


def nothing(k):
    del k


def fetching(sources, buffers, sems, order):
    copies = [
        pltpu.make_async_copy(source, buffer, sems.at[k])
        for k, (source, buffer) in enumerate(zip(sources, buffers))
    ]
    for k in order:
        copies[k].start()
    return lambda k: copies[k].wait()


def forward_kernel(flag, own, far, *refs):
    held, sources, (keep, send, act, total, *buffers, sems) = refs[:3], refs[3:6], refs[6:]
    half = own.shape[0]
    wait = fetching(sources, buffers, sems, (0, 1, 2))

    @pl.when(flag[0] >= 0)
    def _():
        total[...] = forward_half(both(own, far), *held, act.at[0], nothing)

    @pl.when(flag[0] >= 0)
    def _():
        out = total[...] + forward_half(both(own, far), *buffers, act.at[1], wait)
        out = out.astype(jnp.bfloat16)
        keep[...] = out[:half]
        send[...] = out[half:]


def both(own, far):
    return jnp.concatenate([own[...], far[...]], axis=0)


def backward_kernel(flag, own, far, act, *refs):
    held, sources, (keep, send, total, *buffers, sems) = refs[:3], refs[3:6], refs[6:]
    half = own.shape[0]
    wait = fetching(sources, buffers, sems, (2, 0, 1))

    @pl.when(flag[0] >= 0)
    def _():
        total[...] = backward_half(both(own, far), act.at[0], *held, nothing)

    @pl.when(flag[0] >= 0)
    def _():
        grad = total[...] + backward_half(both(own, far), act.at[1], *buffers, wait)
        grad = grad.astype(jnp.bfloat16)
        keep[...] = grad[:half]
        send[...] = grad[half:]


def buffers_of(weights):
    return [pltpu.VMEM(value.shape, value.dtype) for value in weights] + [
        pltpu.SemaphoreType.DMA((len(weights),))
    ]


def forward(flag, own, far, held, fetched_w):
    half, width = own.shape
    part = jax.ShapeDtypeStruct((half, width), jnp.bfloat16)
    act = jax.ShapeDtypeStruct((2, 2, 2 * half, held[0].shape[0]), jnp.float32)
    return pl.pallas_call(
        forward_kernel,
        out_shape=(part, part, act),
        in_specs=[pl.BlockSpec(memory_space=pltpu.SMEM)] + vmem(5) + hbm(3),
        out_specs=tuple(vmem(3)),
        scratch_shapes=[pltpu.VMEM((2 * half, width), jnp.float32)] + buffers_of(fetched_w),
        compiler_params=params(16),
        name="forward",
    )(flag, own, far, *held, *in_hbm(*fetched_w))


def backward(flag, own, far, act, held, fetched_w):
    half, width = own.shape
    part = jax.ShapeDtypeStruct((half, width), jnp.bfloat16)
    return pl.pallas_call(
        backward_kernel,
        out_shape=(part, part),
        in_specs=[pl.BlockSpec(memory_space=pltpu.SMEM)] + vmem(6) + hbm(3),
        out_specs=tuple(vmem(2)),
        scratch_shapes=[pltpu.VMEM((2 * half, width), jnp.float32)] + buffers_of(fetched_w),
        compiler_params=params(16),
        name="backward",
    )(flag, own, far, act, *held, *in_hbm(*fetched_w))


def spread(select, value, exact):
    high = value.astype(jnp.bfloat16)
    chosen = select.astype(jnp.bfloat16)
    total = lax.dot_general(chosen, high, TN, preferred_element_type=jnp.float32)
    if exact:
        return total
    low = (value - high.astype(jnp.float32)).astype(jnp.bfloat16)
    return total + lax.dot_general(chosen, low, TN, preferred_element_type=jnp.float32)


BLOCK = 512


def summed(refs, part):
    total = refs[0][:, part].astype(jnp.float32)
    for other in refs[1:]:
        total = total + other[:, part].astype(jnp.float32)
    return total


def combine_kernel(n_window, parts, *refs):
    outs, grads = refs[:parts], refs[parts : 2 * parts]
    ids, select, slot_prob, slot_cot, layer_out, input_grad, prob_grad = refs[2 * parts : -4]
    out_stage, grad_stage, prob_stage, sems = refs[-4:]
    exact = n_window == 1
    chosen = select[...]
    weight = slot_prob[:, :1]
    width = outs[0].shape[1]
    block = min(BLOCK, width)
    copies = []

    def send(source, target):
        copy = pltpu.make_async_copy(source, target, sems.at[len(copies)])
        copy.start()
        copies.append(copy)

    per_slot = jnp.zeros((chosen.shape[0], 1), jnp.float32)
    for k in range(width // block):
        part = pl.ds(k * block, block)
        out = summed(outs, part)
        per_slot = per_slot + jnp.sum(
            out * slot_cot[:, part].astype(jnp.float32), axis=1, keepdims=True
        )
        out_stage[:, part] = spread(chosen, weight * out, exact).astype(jnp.bfloat16)
        send(out_stage.at[:, part], layer_out.at[:, part])
    spread_prob = chosen * per_slot
    for e in range(n_window):
        per_token = jnp.sum(spread_prob[e * CAP : (e + 1) * CAP], axis=0, keepdims=True)
        kept = jnp.where(ids[...] == e, per_token, 0.0)
        whole = kept if e == 0 else whole + kept
    prob_stage[...] = whole
    send(prob_stage, prob_grad)
    for k in range(width // block):
        part = pl.ds(k * block, block)
        grad_stage[:, part] = spread(chosen, summed(grads, part), exact).astype(jnp.bfloat16)
        send(grad_stage.at[:, part], input_grad.at[:, part])
    for copy in copies:
        copy.wait()


def combine(outs, grads, ids, select, slot_prob, slot_cot, n_window):
    parts = len(outs)
    width = outs[0].shape[1]
    topk, count = ids.shape
    wide = jax.ShapeDtypeStruct((count, width), jnp.bfloat16)
    return pl.pallas_call(
        functools.partial(combine_kernel, n_window, parts),
        out_shape=(wide, wide, jax.ShapeDtypeStruct((topk, count), jnp.float32)),
        in_specs=vmem(2 * parts + 4),
        out_specs=tuple(hbm(3)),
        scratch_shapes=[
            pltpu.VMEM((count, width), jnp.bfloat16),
            pltpu.VMEM((count, width), jnp.bfloat16),
            pltpu.VMEM((topk, count), jnp.float32),
            pltpu.SemaphoreType.DMA((2 * (width // min(BLOCK, width)) + 1,)),
        ],
        compiler_params=params(12),
        name="combine",
    )(*outs, *grads, ids, select, slot_prob, slot_cot)


def chunks(start, size):
    return [(at, min(CHUNK, start + size - at)) for at in range(start, start + size, CHUNK)]


def load(ref, at, size):
    return ref[:, pl.ds(at, size)].astype(jnp.float32)


def row_max(ref, width):
    full, tail = None, None
    for at, span in chunks(0, width):
        value = ref[:, pl.ds(at, span)]
        if span < CHUNK:
            tail = value
        else:
            full = value if full is None else jnp.maximum(full, value)
    tops = [
        jnp.max(value.astype(jnp.float32), axis=1, keepdims=True)
        for value in (full, tail)
        if value is not None
    ]
    return functools.reduce(jnp.maximum, tops)


def row_sums(width, step):
    full = tail = None
    for at, span in chunks(0, width):
        values = step(at, span)
        if span < CHUNK:
            tail = values
        elif full is None:
            full = values
        else:
            full = tuple(one + two for one, two in zip(full, values))
    sums = [jnp.sum(value, axis=1, keepdims=True) for value in (full or tail)]
    if full is not None and tail is not None:
        more = [jnp.sum(value, axis=1, keepdims=True) for value in tail]
        sums = [one + two for one, two in zip(sums, more)]
    return sums


def columns(values, rows):
    lane = lax.broadcasted_iota(jnp.int32, (rows, LANES), 1)
    tile = jnp.zeros((rows, LANES), jnp.float32)
    for k, value in enumerate(values):
        tile = jnp.where(lane == k, value, tile)
    return tile


def diagonal(rows):
    return lax.broadcasted_iota(jnp.int32, (rows, rows), 0) == lax.broadcasted_iota(
        jnp.int32, (rows, rows), 1
    )


def label_kernel(base, labels, out):
    rows = labels.shape[1]
    spread_out = jnp.where(diagonal(rows), jnp.broadcast_to(labels[...], (rows, rows)), 0)
    label = jnp.sum(spread_out.astype(jnp.float32), axis=1, keepdims=True).astype(jnp.int32)
    out[...] = jnp.broadcast_to(label - base[0], out.shape)


def label_columns(base, labels):
    return pl.pallas_call(
        label_kernel,
        out_shape=jax.ShapeDtypeStruct((labels.shape[1], LANES), jnp.int32),
        in_specs=[pl.BlockSpec(memory_space=pltpu.SMEM)] + vmem(1),
        out_specs=vmem(1)[0],
        compiler_params=params(1),
        name="label",
    )(base, labels)


def student_kernel(label_tile, student, stats, power, hit):
    rows, width = student.shape
    label = label_tile[:, 0:1]
    top = row_max(student, width)

    def step(at, size):
        value = load(student, at, size)
        here = lax.broadcasted_iota(jnp.int32, (rows, size), 1) == label - at
        high = jnp.exp(value - top)
        power[:, pl.ds(at, size)] = high
        hit[:, pl.ds(at, size)] = here.astype(jnp.float32)
        return high, jnp.where(here, value, 0.0)

    total, picked = row_sums(width, step)
    zero = jnp.zeros((rows, 1), jnp.float32)
    stats[:rows, :] = columns((top,), rows)
    stats[rows:, :] = columns((total, zero, zero, picked), rows)


def lanes_of(value):
    return [value[:, k : k + LANES] for k in range(0, value.shape[1], LANES)]


def added(values):
    while len(values) > 1:
        pairs = [one + two for one, two in zip(values[::2], values[1::2])]
        values = pairs + values[2 * len(pairs) :]
    return values[0]


def teacher_kernel(student, teacher, student_stats, stats):
    rows, width = student.shape
    top = None
    for at, span in chunks(0, width):
        ours, theirs = lanes_of(load(student, at, span)), lanes_of(load(teacher, at, span))
        ragged = span % LANES
        if ragged:
            pad = jnp.full((rows, LANES - ragged), -jnp.inf, jnp.float32)
            theirs[-1] = jnp.concatenate([theirs[-1], pad], axis=1)
            ours[-1] = jnp.concatenate([ours[-1], jnp.zeros_like(pad)], axis=1)
        high = functools.reduce(jnp.maximum, theirs)
        if top is None:
            total = cross = jnp.zeros((rows, LANES), jnp.float32)
        else:
            high = jnp.maximum(top, high)
            shrink = jnp.exp(top - high)
            total, cross = total * shrink, cross * shrink
        top = high
        powers = [jnp.exp(their - top) for their in theirs]
        gaps = [their - our for our, their in zip(ours, theirs)]
        if ragged:
            gaps[-1] = jnp.where(powers[-1] > 0.0, gaps[-1], 0.0)
        total = total + added(powers)
        cross = cross + added([power * gap for power, gap in zip(powers, gaps)])
    high = jnp.max(top, axis=1, keepdims=True)
    shrink = jnp.exp(top - high)
    total = jnp.sum(total * shrink, axis=1, keepdims=True)
    cross = jnp.sum(cross * shrink, axis=1, keepdims=True)
    top = high
    lane = lax.broadcasted_iota(jnp.int32, (rows, LANES), 1)
    theirs = (lane == 1) | (lane == 2)
    stats[:rows, :] = jnp.where(theirs, top, student_stats[:rows, :])
    value = jnp.where(lane == 1, total, student_stats[rows:, :])
    stats[rows:, :] = jnp.where(lane == 2, cross, value)


def power_kernel(teacher, stats, power):
    top = stats[: teacher.shape[0], 1:2]
    for at, span in chunks(0, teacher.shape[1]):
        power[:, pl.ds(at, span)] = jnp.exp(load(teacher, at, span) - top)


def teacher_power(teacher, stats):
    return pl.pallas_call(
        power_kernel,
        out_shape=jax.ShapeDtypeStruct(teacher.shape, jnp.float32),
        in_specs=vmem(2),
        out_specs=vmem(1)[0],
        compiler_params=params(8),
        name="power",
    )(teacher, stats)


def joined(tiles):
    rows = tiles[0].shape[0] // 2
    tops = [tile[:rows, :] for tile in tiles]
    top = functools.reduce(jnp.maximum, tops)
    parts = [tile[rows:, :] * jnp.exp(one - top) for tile, one in zip(tiles, tops)]
    return top, functools.reduce(jnp.add, parts)


def join_kernel(*refs):
    tiles, out = refs[:-1], refs[-1]
    rows = out.shape[0] // 2
    top, value = joined(tiles)
    out[:rows, :] = top
    out[rows:, :] = value


def join(tiles):
    return pl.pallas_call(
        join_kernel,
        out_shape=jax.ShapeDtypeStruct(tiles[0].shape, tiles[0].dtype),
        in_specs=vmem(len(tiles)),
        out_specs=vmem(1)[0],
        compiler_params=params(1),
        name="join",
    )(*tiles)


def final_kernel(student, teacher, hit, own, *refs):
    tiles, (loss, grad, stage, loss_stage, sems) = refs[:-5], refs[-5:]
    rows, width = student.shape
    top, value = joined(tiles)
    lse = top + jnp.log(value)
    scale = jnp.exp(own[:rows, :] - lse)
    scale_s = 2.0 * scale[:, 0:1]
    scale_t = scale[:, 1:2]
    for at, span in chunks(0, width):
        part = pl.ds(at, span)
        result = student[:, part] * scale_s - teacher[:, part] * scale_t - hit[:, part]
        stage[:, part] = result.astype(jnp.bfloat16)
    grad_copy = pltpu.make_async_copy(stage, grad, sems.at[0])
    grad_copy.start()
    picked, cross = value[:, 3:4], value[:, 2:3]
    total = 2.0 * lse[:, 0:1] - picked + cross / value[:, 1:2] - lse[:, 1:2]
    loss_stage[...] = jnp.sum(jnp.where(diagonal(rows), total, 0.0), axis=0, keepdims=True)
    loss_copy = pltpu.make_async_copy(loss_stage, loss, sems.at[1])
    loss_copy.start()
    grad_copy.wait()
    loss_copy.wait()


def distill(student, teacher, labels):
    base = (lax.axis_index("grp") * student.shape[1]).astype(jnp.int32).reshape(1)
    label = label_columns(base, labels)
    own, power_s, hit = student_stats(label, student)
    stats = teacher_stats(student, teacher, own)
    first = stats
    tiles = exchanged(stats, 1)
    power_t = teacher_power(teacher, stats)
    bits = 4
    while bits < lax.axis_size("grp"):
        stats = join(tiles)
        tiles = exchanged(stats, bits)
        bits = 4 * bits
    return (power_s, power_t, hit, first), tiles


def exchanged(tile, bits):
    tiles = [tile]
    for k in (1, 2, 3):
        if k * bits < lax.axis_size("grp"):
            tiles.append(swapped(tile, "grp", k * bits))
    return tiles


def student_stats(label, student):
    return pl.pallas_call(
        student_kernel,
        out_shape=(
            jax.ShapeDtypeStruct((2 * student.shape[0], LANES), jnp.float32),
            jax.ShapeDtypeStruct(student.shape, jnp.float32),
            jax.ShapeDtypeStruct(student.shape, jnp.float32),
        ),
        in_specs=vmem(2),
        out_specs=tuple(vmem(3)),
        compiler_params=params(8),
        name="student",
    )(label, student)


def teacher_stats(student, teacher, own):
    rows, _ = student.shape
    return pl.pallas_call(
        teacher_kernel,
        out_shape=jax.ShapeDtypeStruct((2 * rows, LANES), jnp.float32),
        in_specs=vmem(3),
        out_specs=vmem(1)[0],
        compiler_params=params(8),
        name="teacher",
    )(student, teacher, own)


def finish(kept, tiles):
    student = kept[0]
    rows = student.shape[0]
    return pl.pallas_call(
        final_kernel,
        out_shape=(
            jax.ShapeDtypeStruct((1, rows), jnp.float32),
            jax.ShapeDtypeStruct(student.shape, jnp.bfloat16),
        ),
        in_specs=vmem(len(kept) + len(tiles)),
        out_specs=tuple(hbm(2)),
        scratch_shapes=[
            pltpu.VMEM(student.shape, jnp.bfloat16),
            pltpu.VMEM((1, rows), jnp.float32),
            pltpu.SemaphoreType.DMA((2,)),
        ],
        compiler_params=params(8),
        name="final",
    )(*kept, *tiles)


def between_blocks(value, n_window):
    if n_window == 1:
        return value
    groups = [[b + PIECES * a for a in range(n_window)] for b in range(PIECES)]
    return lax.all_to_all(
        value, "grp", split_axis=0, concat_axis=0, tiled=True, axis_index_groups=groups
    )


def layer(rows, scaled, slot_cot, select, slot_prob, ids, weights, others, n_window):
    rows = between_blocks(rows, n_window)
    scaled = between_blocks(scaled, n_window)
    rows_far = swapped(rows, "grp", 3)
    scaled_far = swapped(scaled, "grp", 3)
    flag = lax.axis_index("grp").astype(jnp.int32).reshape(1)
    out_keep, out_send, act = forward(flag, rows, rows_far, others, weights)
    out_home = swapped(out_send, "grp", 3)
    grad_keep, grad_send = backward(flag, scaled, scaled_far, act, others, weights)
    grad_home = swapped(grad_send, "grp", 3)

    outs = collected([out_keep, out_home], n_window)
    grads = collected([grad_keep, grad_home], n_window)
    return combine(outs, grads, ids, select, slot_prob, slot_cot, n_window)


def collected(parts, n_window):
    if n_window == 1:
        return parts
    total = functools.reduce(jnp.add, [part.astype(jnp.float32) for part in parts])
    return [between_blocks(total.astype(jnp.bfloat16), n_window)]


def body(
    tokens,
    cotangent,
    expert_ids,
    route_prob,
    w_gate,
    w_up,
    w_down,
    student_logits,
    stale_logits,
    labels,
):
    n_window = lax.axis_size("grp") // PIECES
    teacher = onward(stale_logits[0], "peer")
    rows, select, ids = slot_rows(expert_ids.T, tokens, n_window)
    scaled, slot_cot, slot_prob, labels = slot_scaled(
        ids, select, route_prob.T, cotangent, labels, n_window
    )
    slots = (rows, scaled, slot_cot, select, slot_prob, ids)
    student = student_logits[0]
    weights = (w_gate[0].T, w_up[0].T, w_down[0])
    others = []
    for value in weights:
        others.append(swapped(value, "grp", 1))
    layer_out, input_grad, prob_grad = layer(*slots, weights, others, n_window)
    kept, tiles = distill(student, teacher, labels)
    distill_loss, logit_grad = finish(kept, tiles)
    return (layer_out, input_grad, prob_grad.T, distill_loss, logit_grad[None])


def solution(mesh):
    placed = (
        P(("peer", "grp"), None),
        P(("peer", "grp"), None),
        P(("peer", "grp"), None),
        P(("peer", "grp"), None),
        P("peer", None, "grp"),
        P("peer", None, "grp"),
        P("peer", "grp", None),
        P("peer", None, "grp"),
        P("peer", None, "grp"),
        P("peer", None),
    )
    return jax.shard_map(
        body,
        mesh=mesh,
        in_specs=placed,
        out_specs=(
            P(("peer", "grp"), None),
            P(("peer", "grp"), None),
            P(("peer", "grp"), None),
            P("peer", None),
            P("peer", None, "grp"),
        ),
        check_vma=False,
    )
```

```python
import functools

import jax
import jax.numpy as jnp
from jax import lax
from jax.experimental import pallas as pl
from jax.experimental.pallas import tpu as pltpu
from jax.sharding import PartitionSpec as P


PIECES = 4
CAP = 32
LANES = 128
CHUNK = 2048
NT = (((1,), (1,)), ((), ()))
TN = (((0,), (0,)), ((), ()))


def vmem(count):
    return [pl.BlockSpec(memory_space=pltpu.VMEM)] * count


def hbm(count):
    return [pl.BlockSpec(memory_space=pltpu.HBM)] * count


def in_hbm(*values):
    return [pltpu.with_memory_space_constraint(value, pltpu.HBM) for value in values]


def params(mib):
    return pltpu.CompilerParams(vmem_limit_bytes=mib * 1024 * 1024)


def swapped(value, axis, bits):
    count = lax.axis_size(axis)
    return lax.ppermute(value, axis, [(k, k ^ bits) for k in range(count)])


def onward(value, axis):
    count = lax.axis_size(axis)
    return lax.ppermute(value, axis, [(k, (k + 1) % count) for k in range(count)])


def fetched(sources, buffers, sems):
    copies = [
        pltpu.make_async_copy(source, buffer, sems.at[k])
        for k, (source, buffer) in enumerate(zip(sources, buffers))
    ]
    for copy in copies:
        copy.start()
    return copies


def rows_kernel(n_window, ids_hbm, tokens_hbm, rows, select, ids, tokens, sems):
    copies = fetched((ids_hbm, tokens_hbm), (ids, tokens), sems)
    copies[0].wait()
    all_ids = ids[...]
    count = all_ids.shape[1]
    before = (
        lax.broadcasted_iota(jnp.int32, (count, count), 0)
        < lax.broadcasted_iota(jnp.int32, (count, count), 1)
    ).astype(jnp.float32).astype(jnp.bfloat16)
    slot = lax.broadcasted_iota(jnp.int32, (CAP, count), 0)
    for e in range(n_window):
        part = pl.ds(e * CAP, CAP)
        hit = all_ids == e
        member = jnp.sum(hit.astype(jnp.float32), axis=0, keepdims=True)
        earlier = jnp.dot(
            jnp.broadcast_to(member, (16, count)).astype(jnp.bfloat16),
            before,
            preferred_element_type=jnp.float32,
        )
        position = earlier[:1].astype(jnp.int32)
        chosen = ((slot == position) & (member > 0.5)).astype(jnp.float32)
        select[part, :] = chosen
        if e == 0:
            copies[1].wait()
        rows[part, :] = jnp.dot(
            chosen.astype(jnp.bfloat16), tokens[...], preferred_element_type=jnp.float32
        ).astype(jnp.bfloat16)


def scaled_kernel(n_window, ids, select, prob_hbm, cot_hbm, labels_hbm, *refs):
    scaled, slot_cot, slot_prob, labels, prob, cot, sems = refs
    copies = fetched((prob_hbm, cot_hbm, labels_hbm), (prob, cot, labels), sems)
    copies[0].wait()
    for e in range(n_window):
        part = pl.ds(e * CAP, CAP)
        hit = ids[...] == e
        token_prob = jnp.sum(jnp.where(hit, prob[...], 0.0), axis=0, keepdims=True)
        chosen = select[part, :]
        weight = jnp.sum(chosen * token_prob, axis=1, keepdims=True)
        slot_prob[part, :] = jnp.broadcast_to(weight, (CAP, LANES))
        if e == 0:
            copies[1].wait()
        cot_rows = jnp.dot(
            chosen.astype(jnp.bfloat16), cot[...], preferred_element_type=jnp.float32
        )
        slot_cot[part, :] = cot_rows.astype(jnp.bfloat16)
        scaled[part, :] = (weight * cot_rows).astype(jnp.bfloat16)
    copies[2].wait()


def slot_rows(ids, tokens, n_window):
    count, width = tokens.shape
    slots = n_window * CAP
    return pl.pallas_call(
        functools.partial(rows_kernel, n_window),
        out_shape=(
            jax.ShapeDtypeStruct((slots, width), jnp.bfloat16),
            jax.ShapeDtypeStruct((slots, count), jnp.float32),
            jax.ShapeDtypeStruct(ids.shape, ids.dtype),
        ),
        in_specs=hbm(2),
        out_specs=tuple(vmem(3)),
        scratch_shapes=[
            pltpu.VMEM(tokens.shape, tokens.dtype),
            pltpu.SemaphoreType.DMA((2,)),
        ],
        compiler_params=params(8),
        name="slot_rows",
    )(*in_hbm(ids, tokens))


def slot_scaled(ids, select, prob, cot, labels, n_window):
    slots, width = select.shape[0], cot.shape[1]
    wide = jax.ShapeDtypeStruct((slots, width), jnp.bfloat16)
    return pl.pallas_call(
        functools.partial(scaled_kernel, n_window),
        out_shape=(
            wide,
            wide,
            jax.ShapeDtypeStruct((slots, LANES), jnp.float32),
            jax.ShapeDtypeStruct(labels.shape, labels.dtype),
        ),
        in_specs=vmem(2) + hbm(3),
        out_specs=tuple(vmem(4)),
        scratch_shapes=[
            pltpu.VMEM(prob.shape, prob.dtype),
            pltpu.VMEM(cot.shape, cot.dtype),
            pltpu.SemaphoreType.DMA((3,)),
        ],
        compiler_params=params(8),
        name="slot_scaled",
    )(ids, select, *in_hbm(prob, cot, labels))


def forward_half(rows, gate_w, up_w, down_w, act, wait):
    wait(0)
    gate = lax.dot_general(rows, gate_w[...], NT, preferred_element_type=jnp.float32)
    wait(1)
    up = lax.dot_general(rows, up_w[...], NT, preferred_element_type=jnp.float32)
    act[0] = gate
    act[1] = up
    hidden = (gate * jax.nn.sigmoid(gate) * up).astype(jnp.bfloat16)
    wait(2)
    return jnp.dot(hidden, down_w[...], preferred_element_type=jnp.float32)


def backward_half(scaled, act, gate_w, up_w, down_w, wait):
    gate, up = act[0], act[1]
    sig = jax.nn.sigmoid(gate)
    wait(2)
    grad_hidden = lax.dot_general(scaled, down_w[...], NT, preferred_element_type=jnp.float32)
    grad_gate = (grad_hidden * up * sig * (1.0 + gate * (1.0 - sig))).astype(jnp.bfloat16)
    grad_up = (grad_hidden * gate * sig).astype(jnp.bfloat16)
    wait(0)
    grad = jnp.dot(grad_gate, gate_w[...], preferred_element_type=jnp.float32)
    wait(1)
    return grad + jnp.dot(grad_up, up_w[...], preferred_element_type=jnp.float32)


def nothing(k):
    del k


def fetching(sources, buffers, sems, order):
    copies = [
        pltpu.make_async_copy(source, buffer, sems.at[k])
        for k, (source, buffer) in enumerate(zip(sources, buffers))
    ]
    for k in order:
        copies[k].start()
    return lambda k: copies[k].wait()


def forward_kernel(flag, own, far, *refs):
    held, sources, (keep, send, act, total, *buffers, sems) = refs[:3], refs[3:6], refs[6:]
    half = own.shape[0]
    wait = fetching(sources, buffers, sems, (0, 1, 2))

    @pl.when(flag[0] >= 0)
    def _():
        total[...] = rounded(forward_half(both(own, far), *held, act.at[0], nothing))

    @pl.when(flag[0] >= 0)
    def _():
        out = total[...] + rounded(forward_half(both(own, far), *buffers, act.at[1], wait))
        out = out.astype(jnp.bfloat16)
        keep[...] = out[:half]
        send[...] = out[half:]


def rounded(value):
    return value.astype(jnp.bfloat16).astype(jnp.float32)


def both(own, far):
    return jnp.concatenate([own[...], far[...]], axis=0)


def backward_kernel(flag, own, far, act, *refs):
    held, sources, (keep, send, total, *buffers, sems) = refs[:3], refs[3:6], refs[6:]
    half = own.shape[0]
    wait = fetching(sources, buffers, sems, (2, 0, 1))

    @pl.when(flag[0] >= 0)
    def _():
        total[...] = rounded(backward_half(both(own, far), act.at[0], *held, nothing))

    @pl.when(flag[0] >= 0)
    def _():
        grad = total[...] + rounded(backward_half(both(own, far), act.at[1], *buffers, wait))
        grad = grad.astype(jnp.bfloat16)
        keep[...] = grad[:half]
        send[...] = grad[half:]


def buffers_of(weights):
    return [pltpu.VMEM(value.shape, value.dtype) for value in weights] + [
        pltpu.SemaphoreType.DMA((len(weights),))
    ]


def forward(flag, own, far, held, fetched_w):
    half, width = own.shape
    part = jax.ShapeDtypeStruct((half, width), jnp.bfloat16)
    act = jax.ShapeDtypeStruct((2, 2, 2 * half, held[0].shape[0]), jnp.float32)
    return pl.pallas_call(
        forward_kernel,
        out_shape=(part, part, act),
        in_specs=[pl.BlockSpec(memory_space=pltpu.SMEM)] + vmem(5) + hbm(3),
        out_specs=tuple(vmem(3)),
        scratch_shapes=[pltpu.VMEM((2 * half, width), jnp.float32)] + buffers_of(fetched_w),
        compiler_params=params(16),
        name="forward",
    )(flag, own, far, *held, *in_hbm(*fetched_w))


def backward(flag, own, far, act, held, fetched_w):
    half, width = own.shape
    part = jax.ShapeDtypeStruct((half, width), jnp.bfloat16)
    return pl.pallas_call(
        backward_kernel,
        out_shape=(part, part),
        in_specs=[pl.BlockSpec(memory_space=pltpu.SMEM)] + vmem(6) + hbm(3),
        out_specs=tuple(vmem(2)),
        scratch_shapes=[pltpu.VMEM((2 * half, width), jnp.float32)] + buffers_of(fetched_w),
        compiler_params=params(16),
        name="backward",
    )(flag, own, far, act, *held, *in_hbm(*fetched_w))


def spread(select, value, exact):
    high = value.astype(jnp.bfloat16)
    chosen = select.astype(jnp.bfloat16)
    total = lax.dot_general(chosen, high, TN, preferred_element_type=jnp.float32)
    if exact:
        return total
    low = (value - high.astype(jnp.float32)).astype(jnp.bfloat16)
    return total + lax.dot_general(chosen, low, TN, preferred_element_type=jnp.float32)


BLOCK = 512


def summed(refs, part):
    total = refs[0][:, part].astype(jnp.float32)
    for other in refs[1:]:
        total = total + other[:, part].astype(jnp.float32)
    return total


def combine_kernel(n_window, parts, *refs):
    outs, grads = refs[:parts], refs[parts : 2 * parts]
    ids, select, slot_prob, slot_cot, layer_out, input_grad, prob_grad = refs[2 * parts : -4]
    out_stage, grad_stage, prob_stage, sems = refs[-4:]
    exact = n_window == 1
    chosen = select[...]
    weight = slot_prob[:, :1]
    width = outs[0].shape[1]
    block = min(BLOCK, width)
    copies = []

    def send(source, target):
        copy = pltpu.make_async_copy(source, target, sems.at[len(copies)])
        copy.start()
        copies.append(copy)

    per_slot = jnp.zeros((chosen.shape[0], 1), jnp.float32)
    for k in range(width // block):
        part = pl.ds(k * block, block)
        out = summed(outs, part)
        per_slot = per_slot + jnp.sum(
            out * slot_cot[:, part].astype(jnp.float32), axis=1, keepdims=True
        )
        out_stage[:, part] = spread(chosen, weight * out, exact).astype(jnp.bfloat16)
        send(out_stage.at[:, part], layer_out.at[:, part])
    spread_prob = chosen * per_slot
    for e in range(n_window):
        per_token = jnp.sum(spread_prob[e * CAP : (e + 1) * CAP], axis=0, keepdims=True)
        kept = jnp.where(ids[...] == e, per_token, 0.0)
        whole = kept if e == 0 else whole + kept
    prob_stage[...] = whole
    send(prob_stage, prob_grad)
    for k in range(width // block):
        part = pl.ds(k * block, block)
        grad_stage[:, part] = spread(chosen, summed(grads, part), exact).astype(jnp.bfloat16)
        send(grad_stage.at[:, part], input_grad.at[:, part])
    for copy in copies:
        copy.wait()


def combine(outs, grads, ids, select, slot_prob, slot_cot, n_window):
    parts = len(outs)
    width = outs[0].shape[1]
    topk, count = ids.shape
    wide = jax.ShapeDtypeStruct((count, width), jnp.bfloat16)
    return pl.pallas_call(
        functools.partial(combine_kernel, n_window, parts),
        out_shape=(wide, wide, jax.ShapeDtypeStruct((topk, count), jnp.float32)),
        in_specs=vmem(2 * parts + 4),
        out_specs=tuple(hbm(3)),
        scratch_shapes=[
            pltpu.VMEM((count, width), jnp.bfloat16),
            pltpu.VMEM((count, width), jnp.bfloat16),
            pltpu.VMEM((topk, count), jnp.float32),
            pltpu.SemaphoreType.DMA((2 * (width // min(BLOCK, width)) + 1,)),
        ],
        compiler_params=params(12),
        name="combine",
    )(*outs, *grads, ids, select, slot_prob, slot_cot)


def chunks(start, size):
    return [(at, min(CHUNK, start + size - at)) for at in range(start, start + size, CHUNK)]


def load(ref, at, size):
    return ref[:, pl.ds(at, size)].astype(jnp.float32)


def row_max(ref, width):
    full, tail = None, None
    for at, span in chunks(0, width):
        value = ref[:, pl.ds(at, span)]
        if span < CHUNK:
            tail = value
        else:
            full = value if full is None else jnp.maximum(full, value)
    tops = [
        jnp.max(value.astype(jnp.float32), axis=1, keepdims=True)
        for value in (full, tail)
        if value is not None
    ]
    return functools.reduce(jnp.maximum, tops)


def row_sums(width, step):
    full = tail = None
    for at, span in chunks(0, width):
        values = step(at, span)
        if span < CHUNK:
            tail = values
        elif full is None:
            full = values
        else:
            full = tuple(one + two for one, two in zip(full, values))
    sums = [jnp.sum(value, axis=1, keepdims=True) for value in (full or tail)]
    if full is not None and tail is not None:
        more = [jnp.sum(value, axis=1, keepdims=True) for value in tail]
        sums = [one + two for one, two in zip(sums, more)]
    return sums


def columns(values, rows):
    lane = lax.broadcasted_iota(jnp.int32, (rows, LANES), 1)
    tile = jnp.zeros((rows, LANES), jnp.float32)
    for k, value in enumerate(values):
        tile = jnp.where(lane == k, value, tile)
    return tile


def diagonal(rows):
    return lax.broadcasted_iota(jnp.int32, (rows, rows), 0) == lax.broadcasted_iota(
        jnp.int32, (rows, rows), 1
    )


def label_kernel(base, labels, out):
    rows = labels.shape[1]
    spread_out = jnp.where(diagonal(rows), jnp.broadcast_to(labels[...], (rows, rows)), 0)
    label = jnp.sum(spread_out.astype(jnp.float32), axis=1, keepdims=True).astype(jnp.int32)
    out[...] = jnp.broadcast_to(label - base[0], out.shape)


def label_columns(base, labels):
    return pl.pallas_call(
        label_kernel,
        out_shape=jax.ShapeDtypeStruct((labels.shape[1], LANES), jnp.int32),
        in_specs=[pl.BlockSpec(memory_space=pltpu.SMEM)] + vmem(1),
        out_specs=vmem(1)[0],
        compiler_params=params(1),
        name="label",
    )(base, labels)


def student_kernel(label_tile, student, stats, power, hit):
    rows, width = student.shape
    label = label_tile[:, 0:1]
    top = row_max(student, width)

    def step(at, size):
        value = load(student, at, size)
        here = lax.broadcasted_iota(jnp.int32, (rows, size), 1) == label - at
        high = jnp.exp(value - top)
        power[:, pl.ds(at, size)] = high
        hit[:, pl.ds(at, size)] = here.astype(jnp.float32)
        return high, jnp.where(here, value, 0.0)

    total, picked = row_sums(width, step)
    zero = jnp.zeros((rows, 1), jnp.float32)
    stats[:rows, :] = columns((top,), rows)
    stats[rows:, :] = columns((total, zero, zero, picked), rows)


def lanes_of(value):
    return [value[:, k : k + LANES] for k in range(0, value.shape[1], LANES)]


def added(values):
    while len(values) > 1:
        pairs = [one + two for one, two in zip(values[::2], values[1::2])]
        values = pairs + values[2 * len(pairs) :]
    return values[0]


def teacher_kernel(student, teacher, student_stats, stats):
    rows, width = student.shape
    top = None
    for at, span in chunks(0, width):
        ours, theirs = lanes_of(load(student, at, span)), lanes_of(load(teacher, at, span))
        ragged = span % LANES
        if ragged:
            pad = jnp.full((rows, LANES - ragged), -jnp.inf, jnp.float32)
            theirs[-1] = jnp.concatenate([theirs[-1], pad], axis=1)
            ours[-1] = jnp.concatenate([ours[-1], jnp.zeros_like(pad)], axis=1)
        high = functools.reduce(jnp.maximum, theirs)
        if top is None:
            total = cross = jnp.zeros((rows, LANES), jnp.float32)
        else:
            high = jnp.maximum(top, high)
            shrink = jnp.exp(top - high)
            total, cross = total * shrink, cross * shrink
        top = high
        powers = [jnp.exp(their - top) for their in theirs]
        gaps = [their - our for our, their in zip(ours, theirs)]
        if ragged:
            gaps[-1] = jnp.where(powers[-1] > 0.0, gaps[-1], 0.0)
        total = total + added(powers)
        cross = cross + added([power * gap for power, gap in zip(powers, gaps)])
    high = jnp.max(top, axis=1, keepdims=True)
    shrink = jnp.exp(top - high)
    total = jnp.sum(total * shrink, axis=1, keepdims=True)
    cross = jnp.sum(cross * shrink, axis=1, keepdims=True)
    top = high
    lane = lax.broadcasted_iota(jnp.int32, (rows, LANES), 1)
    theirs = (lane == 1) | (lane == 2)
    stats[:rows, :] = jnp.where(theirs, top, student_stats[:rows, :])
    value = jnp.where(lane == 1, total, student_stats[rows:, :])
    stats[rows:, :] = jnp.where(lane == 2, cross, value)


def power_kernel(teacher, stats, power):
    top = stats[: teacher.shape[0], 1:2]
    for at, span in chunks(0, teacher.shape[1]):
        power[:, pl.ds(at, span)] = jnp.exp(load(teacher, at, span) - top)


def teacher_power(teacher, stats):
    return pl.pallas_call(
        power_kernel,
        out_shape=jax.ShapeDtypeStruct(teacher.shape, jnp.float32),
        in_specs=vmem(2),
        out_specs=vmem(1)[0],
        compiler_params=params(8),
        name="power",
    )(teacher, stats)


def joined(tiles):
    rows = tiles[0].shape[0] // 2
    tops = [tile[:rows, :] for tile in tiles]
    top = functools.reduce(jnp.maximum, tops)
    parts = [tile[rows:, :] * jnp.exp(one - top) for tile, one in zip(tiles, tops)]
    return top, functools.reduce(jnp.add, parts)


def join_kernel(*refs):
    tiles, out = refs[:-1], refs[-1]
    rows = out.shape[0] // 2
    top, value = joined(tiles)
    out[:rows, :] = top
    out[rows:, :] = value


def join(tiles):
    return pl.pallas_call(
        join_kernel,
        out_shape=jax.ShapeDtypeStruct(tiles[0].shape, tiles[0].dtype),
        in_specs=vmem(len(tiles)),
        out_specs=vmem(1)[0],
        compiler_params=params(1),
        name="join",
    )(*tiles)


def final_kernel(flag, student, teacher, hit, own, *refs):
    tiles, (loss, grad, stage, loss_stage, sems) = refs[:-5], refs[-5:]
    rows, width = student.shape
    top, value = joined(tiles)
    lse = top + jnp.log(value)
    scale = jnp.exp(own[:rows, :] - lse)
    scale_s = 2.0 * scale[:, 0:1]
    scale_t = scale[:, 1:2]
    middle = CHUNK * (width // CHUNK // 2)

    def fill(start, stop, k):
        for at, span in chunks(start, stop - start):
            part = pl.ds(at, span)
            result = student[:, part] * scale_s - teacher[:, part] * scale_t - hit[:, part]
            stage[:, part] = result.astype(jnp.bfloat16)
        copy = written(start, stop, k)
        copy.start()

    def written(start, stop, k):
        part = pl.ds(start, stop - start)
        return pltpu.make_async_copy(stage.at[:, part], grad.at[:, part], sems.at[k])

    fill(0, middle, 0)

    @pl.when(flag[0] >= 0)
    def _():
        fill(middle, width, 2)

    picked, cross = value[:, 3:4], value[:, 2:3]
    total = 2.0 * lse[:, 0:1] - picked + cross / value[:, 1:2] - lse[:, 1:2]
    loss_stage[...] = jnp.sum(jnp.where(diagonal(rows), total, 0.0), axis=0, keepdims=True)
    loss_copy = pltpu.make_async_copy(loss_stage, loss, sems.at[1])
    loss_copy.start()
    written(0, middle, 0).wait()
    written(middle, width, 2).wait()
    loss_copy.wait()


def distill(student, teacher, labels):
    base = (lax.axis_index("grp") * student.shape[1]).astype(jnp.int32).reshape(1)
    label = label_columns(base, labels)
    own, power_s, hit = student_stats(label, student)
    stats = teacher_stats(student, teacher, own)
    first = stats
    tiles = exchanged(stats, 1)
    power_t = teacher_power(teacher, stats)
    bits = 4
    while bits < lax.axis_size("grp"):
        stats = join(tiles)
        tiles = exchanged(stats, bits)
        bits = 4 * bits
    return (power_s, power_t, hit, first), tiles


def exchanged(tile, bits):
    tiles = [tile]
    for k in (1, 2, 3):
        if k * bits < lax.axis_size("grp"):
            tiles.append(swapped(tile, "grp", k * bits))
    return tiles


def student_stats(label, student):
    return pl.pallas_call(
        student_kernel,
        out_shape=(
            jax.ShapeDtypeStruct((2 * student.shape[0], LANES), jnp.float32),
            jax.ShapeDtypeStruct(student.shape, jnp.float32),
            jax.ShapeDtypeStruct(student.shape, jnp.float32),
        ),
        in_specs=vmem(2),
        out_specs=tuple(vmem(3)),
        compiler_params=params(8),
        name="student",
    )(label, student)


def teacher_stats(student, teacher, own):
    rows, _ = student.shape
    return pl.pallas_call(
        teacher_kernel,
        out_shape=jax.ShapeDtypeStruct((2 * rows, LANES), jnp.float32),
        in_specs=vmem(3),
        out_specs=vmem(1)[0],
        compiler_params=params(8),
        name="teacher",
    )(student, teacher, own)


def finish(kept, tiles):
    student = kept[0]
    rows = student.shape[0]
    return pl.pallas_call(
        final_kernel,
        out_shape=(
            jax.ShapeDtypeStruct((1, rows), jnp.float32),
            jax.ShapeDtypeStruct(student.shape, jnp.bfloat16),
        ),
        in_specs=[pl.BlockSpec(memory_space=pltpu.SMEM)] + vmem(len(kept) + len(tiles)),
        out_specs=tuple(hbm(2)),
        scratch_shapes=[
            pltpu.VMEM(student.shape, jnp.bfloat16),
            pltpu.VMEM((1, rows), jnp.float32),
            pltpu.SemaphoreType.DMA((3,)),
        ],
        compiler_params=params(8),
        name="final",
    )(lax.axis_index("grp").astype(jnp.int32).reshape(1), *kept, *tiles)


def between_blocks(value, n_window):
    if n_window == 1:
        return value
    groups = [[b + PIECES * a for a in range(n_window)] for b in range(PIECES)]
    return lax.all_to_all(
        value, "grp", split_axis=0, concat_axis=0, tiled=True, axis_index_groups=groups
    )


def layer(rows, scaled, slot_cot, select, slot_prob, ids, weights, others, n_window):
    rows = between_blocks(rows, n_window)
    scaled = between_blocks(scaled, n_window)
    rows_far = swapped(rows, "grp", 3)
    scaled_far = swapped(scaled, "grp", 3)
    flag = lax.axis_index("grp").astype(jnp.int32).reshape(1)
    out_keep, out_send, act = forward(flag, rows, rows_far, others, weights)
    out_home = swapped(out_send, "grp", 3)
    grad_keep, grad_send = backward(flag, scaled, scaled_far, act, others, weights)
    grad_home = swapped(grad_send, "grp", 3)

    outs = collected([out_keep, out_home], n_window)
    grads = collected([grad_keep, grad_home], n_window)
    return combine(outs, grads, ids, select, slot_prob, slot_cot, n_window)


def collected(parts, n_window):
    if n_window == 1:
        return parts
    total = functools.reduce(jnp.add, [part.astype(jnp.float32) for part in parts])
    return [between_blocks(total.astype(jnp.bfloat16), n_window)]


def body(
    tokens,
    cotangent,
    expert_ids,
    route_prob,
    w_gate,
    w_up,
    w_down,
    student_logits,
    stale_logits,
    labels,
):
    n_window = lax.axis_size("grp") // PIECES
    teacher = onward(stale_logits[0], "peer")
    rows, select, ids = slot_rows(expert_ids.T, tokens, n_window)
    scaled, slot_cot, slot_prob, labels = slot_scaled(
        ids, select, route_prob.T, cotangent, labels, n_window
    )
    slots = (rows, scaled, slot_cot, select, slot_prob, ids)
    student = student_logits[0]
    weights = (w_gate[0].T, w_up[0].T, w_down[0])
    others = []
    for value in weights:
        others.append(swapped(value, "grp", 1))
    layer_out, input_grad, prob_grad = layer(*slots, weights, others, n_window)
    kept, tiles = distill(student, teacher, labels)
    distill_loss, logit_grad = finish(kept, tiles)
    return (layer_out, input_grad, prob_grad.T, distill_loss, logit_grad[None])


def solution(mesh):
    placed = (
        P(("peer", "grp"), None),
        P(("peer", "grp"), None),
        P(("peer", "grp"), None),
        P(("peer", "grp"), None),
        P("peer", None, "grp"),
        P("peer", None, "grp"),
        P("peer", "grp", None),
        P("peer", None, "grp"),
        P("peer", None, "grp"),
        P("peer", None),
    )
    return jax.shard_map(
        body,
        mesh=mesh,
        in_specs=placed,
        out_specs=(
            P(("peer", "grp"), None),
            P(("peer", "grp"), None),
            P(("peer", "grp"), None),
            P("peer", None),
            P("peer", None, "grp"),
        ),
        check_vma=False,
    )
```

```python
import functools

import jax
import jax.numpy as jnp
from jax import lax
from jax.experimental import pallas as pl
from jax.experimental.pallas import tpu as pltpu
from jax.sharding import PartitionSpec as P


PIECES = 4
CAP = 32
LANES = 128
CHUNK = 2048
NT = (((1,), (1,)), ((), ()))
TN = (((0,), (0,)), ((), ()))


def vmem(count):
    return [pl.BlockSpec(memory_space=pltpu.VMEM)] * count


def hbm(count):
    return [pl.BlockSpec(memory_space=pltpu.HBM)] * count


def in_hbm(*values):
    return [pltpu.with_memory_space_constraint(value, pltpu.HBM) for value in values]


def params(mib):
    return pltpu.CompilerParams(vmem_limit_bytes=mib * 1024 * 1024)


def swapped(value, axis, bits):
    count = lax.axis_size(axis)
    return lax.ppermute(value, axis, [(k, k ^ bits) for k in range(count)])


def onward(value, axis):
    count = lax.axis_size(axis)
    return lax.ppermute(value, axis, [(k, (k + 1) % count) for k in range(count)])


def fetched(sources, buffers, sems):
    copies = [
        pltpu.make_async_copy(source, buffer, sems.at[k])
        for k, (source, buffer) in enumerate(zip(sources, buffers))
    ]
    for copy in copies:
        copy.start()
    return copies


def rows_kernel(n_window, ids_hbm, tokens_hbm, rows, select, ids, tokens, sems):
    copies = fetched((ids_hbm, tokens_hbm), (ids, tokens), sems)
    copies[0].wait()
    all_ids = ids[...]
    count = all_ids.shape[1]
    before = (
        lax.broadcasted_iota(jnp.int32, (count, count), 0)
        < lax.broadcasted_iota(jnp.int32, (count, count), 1)
    ).astype(jnp.float32).astype(jnp.bfloat16)
    slot = lax.broadcasted_iota(jnp.int32, (CAP, count), 0)
    for e in range(n_window):
        part = pl.ds(e * CAP, CAP)
        hit = all_ids == e
        member = jnp.sum(hit.astype(jnp.float32), axis=0, keepdims=True)
        earlier = jnp.dot(
            jnp.broadcast_to(member, (16, count)).astype(jnp.bfloat16),
            before,
            preferred_element_type=jnp.float32,
        )
        position = earlier[:1].astype(jnp.int32)
        chosen = ((slot == position) & (member > 0.5)).astype(jnp.float32)
        select[part, :] = chosen
        if e == 0:
            copies[1].wait()
        rows[part, :] = jnp.dot(
            chosen.astype(jnp.bfloat16), tokens[...], preferred_element_type=jnp.float32
        ).astype(jnp.bfloat16)


def scaled_kernel(n_window, ids, select, prob_hbm, cot_hbm, labels_hbm, *refs):
    scaled, slot_cot, slot_prob, labels, prob, cot, sems = refs
    copies = fetched((prob_hbm, cot_hbm, labels_hbm), (prob, cot, labels), sems)
    copies[0].wait()
    for e in range(n_window):
        part = pl.ds(e * CAP, CAP)
        hit = ids[...] == e
        token_prob = jnp.sum(jnp.where(hit, prob[...], 0.0), axis=0, keepdims=True)
        chosen = select[part, :]
        weight = jnp.sum(chosen * token_prob, axis=1, keepdims=True)
        slot_prob[part, :] = jnp.broadcast_to(weight, (CAP, LANES))
        if e == 0:
            copies[1].wait()
        cot_rows = jnp.dot(
            chosen.astype(jnp.bfloat16), cot[...], preferred_element_type=jnp.float32
        )
        slot_cot[part, :] = cot_rows.astype(jnp.bfloat16)
        scaled[part, :] = (weight * cot_rows).astype(jnp.bfloat16)
    copies[2].wait()


def slot_rows(ids, tokens, n_window):
    count, width = tokens.shape
    slots = n_window * CAP
    return pl.pallas_call(
        functools.partial(rows_kernel, n_window),
        out_shape=(
            jax.ShapeDtypeStruct((slots, width), jnp.bfloat16),
            jax.ShapeDtypeStruct((slots, count), jnp.float32),
            jax.ShapeDtypeStruct(ids.shape, ids.dtype),
        ),
        in_specs=hbm(2),
        out_specs=tuple(vmem(3)),
        scratch_shapes=[
            pltpu.VMEM(tokens.shape, tokens.dtype),
            pltpu.SemaphoreType.DMA((2,)),
        ],
        compiler_params=params(8),
        name="slot_rows",
    )(*in_hbm(ids, tokens))


def slot_scaled(ids, select, prob, cot, labels, n_window):
    slots, width = select.shape[0], cot.shape[1]
    wide = jax.ShapeDtypeStruct((slots, width), jnp.bfloat16)
    return pl.pallas_call(
        functools.partial(scaled_kernel, n_window),
        out_shape=(
            wide,
            wide,
            jax.ShapeDtypeStruct((slots, LANES), jnp.float32),
            jax.ShapeDtypeStruct(labels.shape, labels.dtype),
        ),
        in_specs=vmem(2) + hbm(3),
        out_specs=tuple(vmem(4)),
        scratch_shapes=[
            pltpu.VMEM(prob.shape, prob.dtype),
            pltpu.VMEM(cot.shape, cot.dtype),
            pltpu.SemaphoreType.DMA((3,)),
        ],
        compiler_params=params(8),
        name="slot_scaled",
    )(ids, select, *in_hbm(prob, cot, labels))


def forward_half(rows, gate_w, up_w, down_w, act, wait):
    wait(0)
    gate = lax.dot_general(rows, gate_w[...], NT, preferred_element_type=jnp.float32)
    wait(1)
    up = lax.dot_general(rows, up_w[...], NT, preferred_element_type=jnp.float32)
    act[0] = gate
    act[1] = up
    hidden = (gate * jax.nn.sigmoid(gate) * up).astype(jnp.bfloat16)
    wait(2)
    return jnp.dot(hidden, down_w[...], preferred_element_type=jnp.float32)


def backward_half(scaled, act, gate_w, up_w, down_w, wait):
    gate, up = act[0], act[1]
    sig = jax.nn.sigmoid(gate)
    wait(2)
    grad_hidden = lax.dot_general(scaled, down_w[...], NT, preferred_element_type=jnp.float32)
    grad_gate = (grad_hidden * up * sig * (1.0 + gate * (1.0 - sig))).astype(jnp.bfloat16)
    grad_up = (grad_hidden * gate * sig).astype(jnp.bfloat16)
    wait(0)
    grad = jnp.dot(grad_gate, gate_w[...], preferred_element_type=jnp.float32)
    wait(1)
    return grad + jnp.dot(grad_up, up_w[...], preferred_element_type=jnp.float32)


def nothing(k):
    del k


def fetching(sources, buffers, sems, order):
    copies = [
        pltpu.make_async_copy(source, buffer, sems.at[k])
        for k, (source, buffer) in enumerate(zip(sources, buffers))
    ]
    for k in order:
        copies[k].start()
    return lambda k: copies[k].wait()


def forward_kernel(flag, own, far, *refs):
    held, sources, (keep, send, act, total, *buffers, sems) = refs[:3], refs[3:6], refs[6:]
    half = own.shape[0]
    wait = fetching(sources, buffers, sems, (0, 1, 2))

    @pl.when(flag[0] >= 0)
    def _():
        total[...] = rounded(forward_half(both(own, far), *held, act.at[0], nothing))

    @pl.when(flag[0] >= 0)
    def _():
        out = total[...] + rounded(forward_half(both(own, far), *buffers, act.at[1], wait))
        keep[...] = out[:half]
        send[...] = out[half:].astype(jnp.bfloat16)


def rounded(value):
    return value.astype(jnp.bfloat16).astype(jnp.float32)


def both(own, far):
    return jnp.concatenate([own[...], far[...]], axis=0)


def backward_kernel(flag, own, far, act, *refs):
    held, sources, (keep, send, total, *buffers, sems) = refs[:3], refs[3:6], refs[6:]
    half = own.shape[0]
    wait = fetching(sources, buffers, sems, (2, 0, 1))

    @pl.when(flag[0] >= 0)
    def _():
        total[...] = rounded(backward_half(both(own, far), act.at[0], *held, nothing))

    @pl.when(flag[0] >= 0)
    def _():
        grad = total[...] + rounded(backward_half(both(own, far), act.at[1], *buffers, wait))
        keep[...] = grad[:half]
        send[...] = grad[half:].astype(jnp.bfloat16)


def buffers_of(weights):
    return [pltpu.VMEM(value.shape, value.dtype) for value in weights] + [
        pltpu.SemaphoreType.DMA((len(weights),))
    ]


def forward(flag, own, far, held, fetched_w):
    half, width = own.shape
    part = jax.ShapeDtypeStruct((half, width), jnp.bfloat16)
    act = jax.ShapeDtypeStruct((2, 2, 2 * half, held[0].shape[0]), jnp.float32)
    return pl.pallas_call(
        forward_kernel,
        out_shape=(jax.ShapeDtypeStruct((half, width), jnp.float32), part, act),
        in_specs=[pl.BlockSpec(memory_space=pltpu.SMEM)] + vmem(5) + hbm(3),
        out_specs=tuple(vmem(3)),
        scratch_shapes=[pltpu.VMEM((2 * half, width), jnp.float32)] + buffers_of(fetched_w),
        compiler_params=params(16),
        name="forward",
    )(flag, own, far, *held, *in_hbm(*fetched_w))


def backward(flag, own, far, act, held, fetched_w):
    half, width = own.shape
    part = jax.ShapeDtypeStruct((half, width), jnp.bfloat16)
    return pl.pallas_call(
        backward_kernel,
        out_shape=(jax.ShapeDtypeStruct((half, width), jnp.float32), part),
        in_specs=[pl.BlockSpec(memory_space=pltpu.SMEM)] + vmem(6) + hbm(3),
        out_specs=tuple(vmem(2)),
        scratch_shapes=[pltpu.VMEM((2 * half, width), jnp.float32)] + buffers_of(fetched_w),
        compiler_params=params(16),
        name="backward",
    )(flag, own, far, act, *held, *in_hbm(*fetched_w))


def spread(select, value, exact):
    high = value.astype(jnp.bfloat16)
    chosen = select.astype(jnp.bfloat16)
    total = lax.dot_general(chosen, high, TN, preferred_element_type=jnp.float32)
    if exact:
        return total
    low = (value - high.astype(jnp.float32)).astype(jnp.bfloat16)
    return total + lax.dot_general(chosen, low, TN, preferred_element_type=jnp.float32)


BLOCK = 512


def summed(refs, part):
    total = refs[0][:, part].astype(jnp.float32)
    for other in refs[1:]:
        total = total + other[:, part].astype(jnp.float32)
    return total


def combine_kernel(n_window, parts, *refs):
    outs, grads = refs[:parts], refs[parts : 2 * parts]
    ids, select, slot_prob, slot_cot, layer_out, input_grad, prob_grad = refs[2 * parts : -4]
    out_stage, grad_stage, prob_stage, sems = refs[-4:]
    exact = n_window == 1
    chosen = select[...]
    weight = slot_prob[:, :1]
    width = outs[0].shape[1]
    block = min(BLOCK, width)
    copies = []

    def send(source, target):
        copy = pltpu.make_async_copy(source, target, sems.at[len(copies)])
        copy.start()
        copies.append(copy)

    per_slot = jnp.zeros((chosen.shape[0], 1), jnp.float32)
    for k in range(width // block):
        part = pl.ds(k * block, block)
        out = summed(outs, part)
        per_slot = per_slot + jnp.sum(
            out * slot_cot[:, part].astype(jnp.float32), axis=1, keepdims=True
        )
        out_stage[:, part] = spread(chosen, weight * out, exact).astype(jnp.bfloat16)
        send(out_stage.at[:, part], layer_out.at[:, part])
    spread_prob = chosen * per_slot
    for e in range(n_window):
        per_token = jnp.sum(spread_prob[e * CAP : (e + 1) * CAP], axis=0, keepdims=True)
        kept = jnp.where(ids[...] == e, per_token, 0.0)
        whole = kept if e == 0 else whole + kept
    prob_stage[...] = whole
    send(prob_stage, prob_grad)
    for k in range(width // block):
        part = pl.ds(k * block, block)
        grad_stage[:, part] = spread(chosen, summed(grads, part), exact).astype(jnp.bfloat16)
        send(grad_stage.at[:, part], input_grad.at[:, part])
    for copy in copies:
        copy.wait()


def combine(outs, grads, ids, select, slot_prob, slot_cot, n_window):
    parts = len(outs)
    width = outs[0].shape[1]
    topk, count = ids.shape
    wide = jax.ShapeDtypeStruct((count, width), jnp.bfloat16)
    return pl.pallas_call(
        functools.partial(combine_kernel, n_window, parts),
        out_shape=(wide, wide, jax.ShapeDtypeStruct((topk, count), jnp.float32)),
        in_specs=vmem(2 * parts + 4),
        out_specs=tuple(hbm(3)),
        scratch_shapes=[
            pltpu.VMEM((count, width), jnp.bfloat16),
            pltpu.VMEM((count, width), jnp.bfloat16),
            pltpu.VMEM((topk, count), jnp.float32),
            pltpu.SemaphoreType.DMA((2 * (width // min(BLOCK, width)) + 1,)),
        ],
        compiler_params=params(12),
        name="combine",
    )(*outs, *grads, ids, select, slot_prob, slot_cot)


def chunks(start, size):
    return [(at, min(CHUNK, start + size - at)) for at in range(start, start + size, CHUNK)]


def load(ref, at, size):
    return ref[:, pl.ds(at, size)].astype(jnp.float32)


def row_max(ref, width):
    full, tail = None, None
    for at, span in chunks(0, width):
        value = ref[:, pl.ds(at, span)]
        if span < CHUNK:
            tail = value
        else:
            full = value if full is None else jnp.maximum(full, value)
    tops = [
        jnp.max(value.astype(jnp.float32), axis=1, keepdims=True)
        for value in (full, tail)
        if value is not None
    ]
    return functools.reduce(jnp.maximum, tops)


def row_sums(width, step):
    full = tail = None
    for at, span in chunks(0, width):
        values = step(at, span)
        if span < CHUNK:
            tail = values
        elif full is None:
            full = values
        else:
            full = tuple(one + two for one, two in zip(full, values))
    sums = [jnp.sum(value, axis=1, keepdims=True) for value in (full or tail)]
    if full is not None and tail is not None:
        more = [jnp.sum(value, axis=1, keepdims=True) for value in tail]
        sums = [one + two for one, two in zip(sums, more)]
    return sums


def columns(values, rows):
    lane = lax.broadcasted_iota(jnp.int32, (rows, LANES), 1)
    tile = jnp.zeros((rows, LANES), jnp.float32)
    for k, value in enumerate(values):
        tile = jnp.where(lane == k, value, tile)
    return tile


def diagonal(rows):
    return lax.broadcasted_iota(jnp.int32, (rows, rows), 0) == lax.broadcasted_iota(
        jnp.int32, (rows, rows), 1
    )


def label_kernel(base, labels, out):
    rows = labels.shape[1]
    spread_out = jnp.where(diagonal(rows), jnp.broadcast_to(labels[...], (rows, rows)), 0)
    label = jnp.sum(spread_out.astype(jnp.float32), axis=1, keepdims=True).astype(jnp.int32)
    out[...] = jnp.broadcast_to(label - base[0], out.shape)


def label_columns(base, labels):
    return pl.pallas_call(
        label_kernel,
        out_shape=jax.ShapeDtypeStruct((labels.shape[1], LANES), jnp.int32),
        in_specs=[pl.BlockSpec(memory_space=pltpu.SMEM)] + vmem(1),
        out_specs=vmem(1)[0],
        compiler_params=params(1),
        name="label",
    )(base, labels)


def student_kernel(label_tile, student, stats, power, hit):
    rows, width = student.shape
    label = label_tile[:, 0:1]
    top = row_max(student, width)

    def step(at, size):
        value = load(student, at, size)
        here = lax.broadcasted_iota(jnp.int32, (rows, size), 1) == label - at
        high = jnp.exp(value - top)
        power[:, pl.ds(at, size)] = high
        hit[:, pl.ds(at, size)] = here.astype(jnp.float32)
        return high, jnp.where(here, value, 0.0)

    total, picked = row_sums(width, step)
    zero = jnp.zeros((rows, 1), jnp.float32)
    stats[:rows, :] = columns((top,), rows)
    stats[rows:, :] = columns((total, zero, zero, picked), rows)


def lanes_of(value):
    return [value[:, k : k + LANES] for k in range(0, value.shape[1], LANES)]


def added(values):
    while len(values) > 1:
        pairs = [one + two for one, two in zip(values[::2], values[1::2])]
        values = pairs + values[2 * len(pairs) :]
    return values[0]


def teacher_kernel(student, teacher, student_stats, stats):
    rows, width = student.shape
    top = None
    for at, span in chunks(0, width):
        ours, theirs = lanes_of(load(student, at, span)), lanes_of(load(teacher, at, span))
        ragged = span % LANES
        if ragged:
            pad = jnp.full((rows, LANES - ragged), -jnp.inf, jnp.float32)
            theirs[-1] = jnp.concatenate([theirs[-1], pad], axis=1)
            ours[-1] = jnp.concatenate([ours[-1], jnp.zeros_like(pad)], axis=1)
        high = functools.reduce(jnp.maximum, theirs)
        if top is None:
            total = cross = jnp.zeros((rows, LANES), jnp.float32)
        else:
            high = jnp.maximum(top, high)
            shrink = jnp.exp(top - high)
            total, cross = total * shrink, cross * shrink
        top = high
        powers = [jnp.exp(their - top) for their in theirs]
        gaps = [their - our for our, their in zip(ours, theirs)]
        if ragged:
            gaps[-1] = jnp.where(powers[-1] > 0.0, gaps[-1], 0.0)
        total = total + added(powers)
        cross = cross + added([power * gap for power, gap in zip(powers, gaps)])
    high = jnp.max(top, axis=1, keepdims=True)
    shrink = jnp.exp(top - high)
    total = jnp.sum(total * shrink, axis=1, keepdims=True)
    cross = jnp.sum(cross * shrink, axis=1, keepdims=True)
    top = high
    lane = lax.broadcasted_iota(jnp.int32, (rows, LANES), 1)
    theirs = (lane == 1) | (lane == 2)
    stats[:rows, :] = jnp.where(theirs, top, student_stats[:rows, :])
    value = jnp.where(lane == 1, total, student_stats[rows:, :])
    stats[rows:, :] = jnp.where(lane == 2, cross, value)


def power_kernel(teacher, stats, power):
    top = stats[: teacher.shape[0], 1:2]
    for at, span in chunks(0, teacher.shape[1]):
        power[:, pl.ds(at, span)] = jnp.exp(load(teacher, at, span) - top)


def teacher_power(teacher, stats):
    return pl.pallas_call(
        power_kernel,
        out_shape=jax.ShapeDtypeStruct(teacher.shape, jnp.float32),
        in_specs=vmem(2),
        out_specs=vmem(1)[0],
        compiler_params=params(8),
        name="power",
    )(teacher, stats)


def joined(tiles):
    rows = tiles[0].shape[0] // 2
    tops = [tile[:rows, :] for tile in tiles]
    top = functools.reduce(jnp.maximum, tops)
    parts = [tile[rows:, :] * jnp.exp(one - top) for tile, one in zip(tiles, tops)]
    return top, functools.reduce(jnp.add, parts)


def join_kernel(*refs):
    tiles, out = refs[:-1], refs[-1]
    rows = out.shape[0] // 2
    top, value = joined(tiles)
    out[:rows, :] = top
    out[rows:, :] = value


def join(tiles):
    return pl.pallas_call(
        join_kernel,
        out_shape=jax.ShapeDtypeStruct(tiles[0].shape, tiles[0].dtype),
        in_specs=vmem(len(tiles)),
        out_specs=vmem(1)[0],
        compiler_params=params(1),
        name="join",
    )(*tiles)


def final_kernel(flag, student, teacher, hit, own, *refs):
    tiles, (loss, grad, stage, loss_stage, sems) = refs[:-5], refs[-5:]
    rows, width = student.shape
    top, value = joined(tiles)
    lse = top + jnp.log(value)
    scale = jnp.exp(own[:rows, :] - lse)
    scale_s = 2.0 * scale[:, 0:1]
    scale_t = scale[:, 1:2]
    middle = CHUNK * (width // CHUNK // 2)

    def fill(start, stop, k):
        for at, span in chunks(start, stop - start):
            part = pl.ds(at, span)
            result = student[:, part] * scale_s - teacher[:, part] * scale_t - hit[:, part]
            stage[:, part] = result.astype(jnp.bfloat16)
        copy = written(start, stop, k)
        copy.start()

    def written(start, stop, k):
        part = pl.ds(start, stop - start)
        return pltpu.make_async_copy(stage.at[:, part], grad.at[:, part], sems.at[k])

    fill(0, middle, 0)

    @pl.when(flag[0] >= 0)
    def _():
        fill(middle, width, 2)

    picked, cross = value[:, 3:4], value[:, 2:3]
    total = 2.0 * lse[:, 0:1] - picked + cross / value[:, 1:2] - lse[:, 1:2]
    loss_stage[...] = jnp.sum(jnp.where(diagonal(rows), total, 0.0), axis=0, keepdims=True)
    loss_copy = pltpu.make_async_copy(loss_stage, loss, sems.at[1])
    loss_copy.start()
    written(0, middle, 0).wait()
    written(middle, width, 2).wait()
    loss_copy.wait()


def distill(student, teacher, labels):
    base = (lax.axis_index("grp") * student.shape[1]).astype(jnp.int32).reshape(1)
    label = label_columns(base, labels)
    own, power_s, hit = student_stats(label, student)
    stats = teacher_stats(student, teacher, own)
    first = stats
    tiles = exchanged(stats, 1)
    power_t = teacher_power(teacher, stats)
    bits = 4
    while bits < lax.axis_size("grp"):
        stats = join(tiles)
        tiles = exchanged(stats, bits)
        bits = 4 * bits
    return (power_s, power_t, hit, first), tiles


def exchanged(tile, bits):
    tiles = [tile]
    for k in (1, 2, 3):
        if k * bits < lax.axis_size("grp"):
            tiles.append(swapped(tile, "grp", k * bits))
    return tiles


def student_stats(label, student):
    return pl.pallas_call(
        student_kernel,
        out_shape=(
            jax.ShapeDtypeStruct((2 * student.shape[0], LANES), jnp.float32),
            jax.ShapeDtypeStruct(student.shape, jnp.float32),
            jax.ShapeDtypeStruct(student.shape, jnp.float32),
        ),
        in_specs=vmem(2),
        out_specs=tuple(vmem(3)),
        compiler_params=params(8),
        name="student",
    )(label, student)


def teacher_stats(student, teacher, own):
    rows, _ = student.shape
    return pl.pallas_call(
        teacher_kernel,
        out_shape=jax.ShapeDtypeStruct((2 * rows, LANES), jnp.float32),
        in_specs=vmem(3),
        out_specs=vmem(1)[0],
        compiler_params=params(8),
        name="teacher",
    )(student, teacher, own)


def finish(kept, tiles):
    student = kept[0]
    rows = student.shape[0]
    return pl.pallas_call(
        final_kernel,
        out_shape=(
            jax.ShapeDtypeStruct((1, rows), jnp.float32),
            jax.ShapeDtypeStruct(student.shape, jnp.bfloat16),
        ),
        in_specs=[pl.BlockSpec(memory_space=pltpu.SMEM)] + vmem(len(kept) + len(tiles)),
        out_specs=tuple(hbm(2)),
        scratch_shapes=[
            pltpu.VMEM(student.shape, jnp.bfloat16),
            pltpu.VMEM((1, rows), jnp.float32),
            pltpu.SemaphoreType.DMA((3,)),
        ],
        compiler_params=params(8),
        name="final",
    )(lax.axis_index("grp").astype(jnp.int32).reshape(1), *kept, *tiles)


def between_blocks(value, n_window):
    if n_window == 1:
        return value
    groups = [[b + PIECES * a for a in range(n_window)] for b in range(PIECES)]
    return lax.all_to_all(
        value, "grp", split_axis=0, concat_axis=0, tiled=True, axis_index_groups=groups
    )


def layer(rows, scaled, slot_cot, select, slot_prob, ids, weights, others, n_window):
    rows = between_blocks(rows, n_window)
    scaled = between_blocks(scaled, n_window)
    rows_far = swapped(rows, "grp", 3)
    scaled_far = swapped(scaled, "grp", 3)
    flag = lax.axis_index("grp").astype(jnp.int32).reshape(1)
    out_keep, out_send, act = forward(flag, rows, rows_far, others, weights)
    out_home = swapped(out_send, "grp", 3)
    grad_keep, grad_send = backward(flag, scaled, scaled_far, act, others, weights)
    grad_home = swapped(grad_send, "grp", 3)

    outs = collected([out_keep, out_home], n_window)
    grads = collected([grad_keep, grad_home], n_window)
    return combine(outs, grads, ids, select, slot_prob, slot_cot, n_window)


def collected(parts, n_window):
    if n_window == 1:
        return parts
    total = functools.reduce(jnp.add, [part.astype(jnp.float32) for part in parts])
    return [between_blocks(total.astype(jnp.bfloat16), n_window)]


def body(
    tokens,
    cotangent,
    expert_ids,
    route_prob,
    w_gate,
    w_up,
    w_down,
    student_logits,
    stale_logits,
    labels,
):
    n_window = lax.axis_size("grp") // PIECES
    teacher = onward(stale_logits[0], "peer")
    rows, select, ids = slot_rows(expert_ids.T, tokens, n_window)
    scaled, slot_cot, slot_prob, labels = slot_scaled(
        ids, select, route_prob.T, cotangent, labels, n_window
    )
    slots = (rows, scaled, slot_cot, select, slot_prob, ids)
    student = student_logits[0]
    weights = (w_gate[0].T, w_up[0].T, w_down[0])
    others = []
    for value in weights:
        others.append(swapped(value, "grp", 1))
    layer_out, input_grad, prob_grad = layer(*slots, weights, others, n_window)
    kept, tiles = distill(student, teacher, labels)
    distill_loss, logit_grad = finish(kept, tiles)
    return (layer_out, input_grad, prob_grad.T, distill_loss, logit_grad[None])


def solution(mesh):
    placed = (
        P(("peer", "grp"), None),
        P(("peer", "grp"), None),
        P(("peer", "grp"), None),
        P(("peer", "grp"), None),
        P("peer", None, "grp"),
        P("peer", None, "grp"),
        P("peer", "grp", None),
        P("peer", None, "grp"),
        P("peer", None, "grp"),
        P("peer", None),
    )
    return jax.shard_map(
        body,
        mesh=mesh,
        in_specs=placed,
        out_specs=(
            P(("peer", "grp"), None),
            P(("peer", "grp"), None),
            P(("peer", "grp"), None),
            P("peer", None),
            P("peer", None, "grp"),
        ),
        check_vma=False,
    )
```
